256 devices in a mesh: seq: 32 (over z, x_hi, core), kv: 8 (over x_lo, y).
Axes of the slice: x: 4 (x_hi: 2, x_lo: 2; x = x_hi * 2 + x_lo), y: 4, z: 8, core: 2. Of those that a mesh axis runs over, the one named last changes fastest.
Arguments:
- queries: bfloat16 [4096, 8192], P('seq', 'kv'), may hold values from -60 to 60
- keys: bfloat16 [4096, 1024], P('seq', 'kv'), may hold values from -8 to 8
- values: bfloat16 [4096, 1024], P('seq', 'kv'), may hold values from -6 to 6
- out_weight: bfloat16 [8192, 8192], P(None, ('kv', 'seq')), may hold values from -0.0625 to 0.0625
- out_grad: bfloat16 [4096, 8192], P('seq', 'kv'), may hold values from -6 to 6
- doc_ids: int32 [4096], P('seq'), may hold values from 0 to 6, never falling along the last dimension, each value on 1 to 1152 neighbouring positions
- block_mask: int32 [32, 32], P('seq'), may hold values 0 or 1
- positions: int32 [3, 4096], P(None, 'seq'), may hold values from 0 to 1023
Outputs:
- layer_out: bfloat16 [4096, 8192], P('seq', 'kv')
- query_grad: bfloat16 [4096, 8192], P('seq', 'kv')
- key_grad: bfloat16 [4096, 1024], P('seq', 'kv')
- value_grad: bfloat16 [4096, 1024], P('seq', 'kv')
The draws below stay inside these ranges and needn't reach their ends.
Inputs may be any that keep to these rules, and one draw needn't show every extreme that they name: `doc_ids`: every document has at most 1152 tokens, and one has exactly 1152.
All inputs are finite; a program needn't handle non-finite values. No bound on the sum of `block_mask` on one device may be relied on, other than what follows from the above.
Results may differ from the reference program's by a relative error of at most 0.017.
Values may be sent and summed in bfloat16 or wider, within the bound.
A program may use at most 128 MiB of HBM per device.

```python
import math
import jax
import jax.numpy as jnp
import numpy as np
from jax import lax

D = 8192
HD = 128
QPG = 8
KV_DEV = 1
TOK_DEV = 128
BLK = 128
REACH = 9
SEQ_LEN = 4096
KVH = 8
QH = 64
DOCMAX = 1152
NBLK = 32
N_SEQ = 32
N_KV = 8


def paired_draw(key):
    base = jax.random.fold_in(key, 911)
    key_part = jax.random.normal(jax.random.fold_in(base, 1), (SEQ_LEN, KVH, HD), jnp.float32)
    query_part = jax.random.normal(jax.random.fold_in(base, 2), (SEQ_LEN, KVH, QPG, HD), jnp.float32)
    query_part = jnp.clip(query_part, -60.0, 60.0)
    key_part = jnp.clip(key_part, -8.0, 8.0)
    return (query_part.reshape(SEQ_LEN, QH * HD), key_part.reshape(SEQ_LEN, KVH * HD))


def draw_queries(key, part):
    return paired_draw(key)[0].astype(jnp.bfloat16)


def draw_keys(key, part):
    return paired_draw(key)[1].astype(jnp.bfloat16)


def plant(drawn, rng, smallest, high):
    extent = drawn.shape
    spot = [jax.random.randint(jax.random.fold_in(rng, axis), (), 0, extent[axis]) for axis in range(len(extent))]
    drawn = drawn.at[tuple(spot)].set(smallest)
    longest = extent.index(max(extent))
    spot[longest] = (spot[longest] + 1) % extent[longest]
    return drawn.at[tuple(spot)].set(high)


def block_levels(stream_key, extent, shards, least, largest):
    factor_of = 1.0
    for axis_at, blocks in shards:
        draws = jax.random.uniform(jax.random.fold_in(jax.random.fold_in(stream_key, 6), axis_at), (blocks,), jnp.float32, least / len(shards), largest / len(shards))
        factor_of = factor_of * jnp.repeat(jnp.exp(draws), extent[axis_at] // blocks).reshape((-1,) + (1,) * (len(extent) - 1 - axis_at))
    return factor_of


def profile(count, total, reach, skew):
    portions = [(1 << 20) // math.isqrt(standing ** skew) + 1 for standing in range(2, count + 1)]
    surplus, given = total - reach - (count - 1), [1] * (count - 1)
    while surplus > 0:
        movable = [i for i in range(count - 1) if given[i] < reach]
        mass, left = sum([portions[i] for i in movable]), surplus
        for i in movable:
            extra = min(reach - given[i], max(1, left * portions[i] // mass), surplus)
            given[i] = given[i] + extra
            surplus = surplus - extra
    return np.array([reach] + given)


def ragged(own_key, amount, total, bound, lean):
    if amount == 2:
        one = jax.random.randint(own_key, (), max(1, total - bound), min(bound, total - 1) + 1)
        return jnp.stack([one, total - one])
    sizes = jnp.asarray(profile(amount, total, bound, lean), jnp.int32)
    pairs = (amount - 1) // 2
    donor, sink = sizes[1:1 + 2 * pairs:2], sizes[2:2 + 2 * pairs:2]
    slack = jnp.minimum(donor - 1, bound - sink)
    passed = jax.random.randint(jax.random.fold_in(own_key, 1), (pairs,), 0, 1 << 20) % (slack + 1)
    sizes = sizes.at[1:1 + 2 * pairs:2].set(donor - passed).at[2:2 + 2 * pairs:2].set(sink + passed)
    return sizes[jax.random.permutation(jax.random.fold_in(own_key, 2), amount)]


def gaussian(key, shape, deviation, reach, pieces=(), kind=jnp.bfloat16):
    drawn = jax.random.normal(key, shape, jnp.float32) * deviation
    if len(pieces) > 0:
        drawn = block_levels(key, shape, pieces, -0.22, 0.18) * drawn
    return jnp.clip(drawn, min=-reach, max=reach).astype(kind)


def setup_inputs(seed: int = 0) -> dict:
    splits = jax.random.split(jax.random.key(seed), 9)
    return {
        "queries": draw_queries(jax.random.fold_in(splits[8], 71), 0),
        "keys": draw_keys(jax.random.fold_in(splits[8], 71), 0),
        "values": gaussian(splits[2], (SEQ_LEN, KVH * HD), 1.0, 6.0, ((0, 32), (1, 8))),
        "out_weight": gaussian(splits[3], (QH * HD, D), (QH * HD) ** -0.5, 0.0625, ((1, 256),)),
        "out_grad": gaussian(splits[4], (SEQ_LEN, D), 1.0, 6.0, ((0, 32), (1, 8))),
        "doc_ids": jnp.searchsorted(jnp.cumsum(ragged(splits[5], 2 * SEQ_LEN // DOCMAX, SEQ_LEN, DOCMAX, 2)), jnp.arange(SEQ_LEN), side="right").astype(jnp.int32),
        "block_mask": plant((jax.random.randint(splits[6], (NBLK, NBLK), 0, 4) < 3).astype(jnp.int32), jax.random.fold_in(splits[6], 1), 0, 1),
        "positions": plant(jax.random.randint(splits[7], (3, SEQ_LEN), 0, 1024), jax.random.fold_in(splits[7], 1), 0, 1023).astype(jnp.int32),
    }


rope_base = 1000000.0


def rope_tables(positions):
    pairs = HD // 2
    index = jnp.arange(pairs)
    inv_freq = jnp.exp(index.astype(jnp.float32) * (-2.0 * math.log(rope_base) / HD))
    temporal = HD // 8
    which = jnp.where(index >= pairs - temporal, 0, jnp.where(index % 2 == 0, 1, 2))
    places = positions.astype(jnp.float32)
    chosen = jnp.where((which == 0)[:, None], places[0][None, :], 0.0)
    chosen = chosen + jnp.where((which == 1)[:, None], places[1][None, :], 0.0)
    chosen = chosen + jnp.where((which == 2)[:, None], places[2][None, :], 0.0)
    angle = chosen.T * inv_freq[None, :]
    return jnp.cos(angle), jnp.sin(angle)


def rotate(block, cosine, sine, sign):
    half = HD // 2
    first = block[..., :half]
    second = block[..., half:]
    cos_part = cosine[:, None, :]
    sin_part = sine[:, None, :] * sign
    return jnp.concatenate([first * cos_part - second * sin_part, second * cos_part + first * sin_part], axis=-1)


def allowed_mask(shard, doc_query, doc_key, mask_rows):
    length = doc_query.shape[0]
    width = doc_key.shape[0]
    query_pos = shard * length + jnp.arange(length, dtype=jnp.int32)
    key_pos = (shard - REACH) * length + jnp.arange(width, dtype=jnp.int32)
    near = jnp.repeat(jnp.repeat(mask_rows, BLK, axis=0), BLK, axis=1) > 0
    same_block = (query_pos[:, None] // BLK) == (key_pos[None, :] // BLK)
    return (doc_query[:, None] == doc_key[None, :]) & (key_pos[None, :] <= query_pos[:, None]) & (key_pos[None, :] >= 0) & (near | same_block)


def attend(query, key_win, value_win, allowed, grad_out):
    scale = HD ** -0.5
    contract = (((1,), (1,)), ((), ()))
    columns = (((0,), (0,)), ((), ()))
    scores = lax.dot_general(query, key_win, contract, preferred_element_type=jnp.float32) * scale
    scores = jnp.where(allowed, scores, -1e30)
    top = jnp.max(scores, axis=1, keepdims=True)
    expo = jnp.exp(scores - top)
    weights = (expo / jnp.sum(expo, axis=1, keepdims=True)).astype(jnp.bfloat16)
    output = jnp.dot(weights, value_win, preferred_element_type=jnp.float32).astype(jnp.bfloat16)
    delta = jnp.sum(grad_out.astype(jnp.float32) * output.astype(jnp.float32), axis=1, keepdims=True)
    dprob = lax.dot_general(grad_out, value_win, contract, preferred_element_type=jnp.float32)
    dscore = (weights.astype(jnp.float32) * (dprob - delta)).astype(jnp.bfloat16)
    dquery = jnp.dot(dscore, key_win, preferred_element_type=jnp.float32) * scale
    dkey = lax.dot_general(dscore, query, columns, preferred_element_type=jnp.float32) * scale
    dvalue = lax.dot_general(weights, grad_out, columns, preferred_element_type=jnp.float32)
    return output, dquery, dkey, dvalue


def reference(queries, keys, values, out_weight, out_grad, doc_ids, block_mask, positions):
    window = (REACH + 1) * TOK_DEV
    blocks_dev = TOK_DEV // BLK
    cosine, sine = rope_tables(positions)
    q_rot = rotate(queries.astype(jnp.float32).reshape(SEQ_LEN, QH, HD), cosine, sine, 1.0).astype(jnp.bfloat16)
    k_rot = rotate(keys.astype(jnp.float32).reshape(SEQ_LEN, KVH, HD), cosine, sine, 1.0).astype(jnp.bfloat16)
    head_grad = lax.dot_general(out_grad, out_weight, (((1,), (1,)), ((), ())), preferred_element_type=jnp.float32).astype(jnp.bfloat16).reshape(SEQ_LEN, QH, HD)
    margin = REACH * TOK_DEV
    k_pad = jnp.pad(k_rot, ((margin, 0), (0, 0), (0, 0)))
    v_pad = jnp.pad(values.reshape(SEQ_LEN, KVH, HD), ((margin, 0), (0, 0), (0, 0)))
    doc_pad = jnp.pad(doc_ids, (margin, 0), constant_values=-1)
    mask_pad = jnp.pad(block_mask, ((0, 0), (REACH * blocks_dev, 0)))

    def shard_step(carry, shard):
        dk_acc, dv_acc = carry
        start = (shard * TOK_DEV).astype(jnp.int32)
        query_blk = lax.dynamic_slice_in_dim(q_rot, start, TOK_DEV, 0)
        grad_blk = lax.dynamic_slice_in_dim(head_grad, start, TOK_DEV, 0)
        key_win = lax.dynamic_slice_in_dim(k_pad, start, window, 0)
        value_win = lax.dynamic_slice_in_dim(v_pad, start, window, 0)
        doc_key = lax.dynamic_slice_in_dim(doc_pad, start, window, 0)
        doc_query = lax.dynamic_slice_in_dim(doc_ids, start, TOK_DEV, 0)
        mask_rows = lax.dynamic_slice(mask_pad, ((shard * blocks_dev).astype(jnp.int32), (shard * blocks_dev).astype(jnp.int32)), (blocks_dev, (REACH + 1) * blocks_dev))
        allowed = allowed_mask(shard, doc_query, doc_key, mask_rows)
        outputs = []
        dqueries = []
        dkeys = []
        dvalues = []
        for group in range(KVH):
            dkey_sum = jnp.zeros((window, HD), jnp.float32)
            dvalue_sum = jnp.zeros((window, HD), jnp.float32)
            for inner in range(QPG):
                head = group * QPG + inner
                output, dquery, dkey, dvalue = attend(query_blk[:, head], key_win[:, group], value_win[:, group], allowed, grad_blk[:, head])
                outputs.append(output)
                dqueries.append(dquery)
                dkey_sum = dkey_sum + dkey
                dvalue_sum = dvalue_sum + dvalue
            dkeys.append(dkey_sum)
            dvalues.append(dvalue_sum)
        dk_win = jnp.stack(dkeys, axis=1)
        dv_win = jnp.stack(dvalues, axis=1)
        dk_acc = lax.dynamic_update_slice_in_dim(dk_acc, lax.dynamic_slice_in_dim(dk_acc, start, window, 0) + dk_win, start, 0)
        dv_acc = lax.dynamic_update_slice_in_dim(dv_acc, lax.dynamic_slice_in_dim(dv_acc, start, window, 0) + dv_win, start, 0)
        return (dk_acc, dv_acc), (jnp.concatenate(outputs, axis=1), jnp.stack(dqueries, axis=1))

    zeros = jnp.zeros((margin + SEQ_LEN, KVH, HD), jnp.float32)
    (dk_acc, dv_acc), (attn, dq_rot) = lax.scan(shard_step, (zeros, zeros), jnp.arange(N_SEQ, dtype=jnp.int32))
    attn = attn.reshape(SEQ_LEN, QH * HD)
    dq_rot = dq_rot.reshape(SEQ_LEN, QH, HD)
    rows = KV_DEV * QPG * HD
    total = jnp.zeros((SEQ_LEN, D), jnp.float32)
    for group in range(N_KV):
        part = jnp.dot(attn[:, group * rows:(group + 1) * rows], out_weight[group * rows:(group + 1) * rows], preferred_element_type=jnp.float32).astype(jnp.bfloat16)
        part = lax.optimization_barrier(part)
        total = total + part.astype(jnp.float32)
    layer_out = total.astype(jnp.bfloat16)
    query_grad = rotate(dq_rot, cosine, sine, -1.0).astype(jnp.bfloat16).reshape(SEQ_LEN, QH * HD)
    key_grad = rotate(dk_acc[margin:], cosine, sine, -1.0).astype(jnp.bfloat16).reshape(SEQ_LEN, KVH * HD)
    value_grad = dv_acc[margin:].astype(jnp.bfloat16).reshape(SEQ_LEN, KVH * HD)
    return (layer_out, query_grad, key_grad, value_grad)
```

```python
import math

import jax
import jax.numpy as jnp
from jax import lax
from jax.sharding import Mesh
from jax.sharding import PartitionSpec as P

HD = 128
BLK = 128
REACH = 9

SEQ = ("sz", "core")

rope_base = 1000000.0


def seq_size():
    return lax.axis_size("sz") * lax.axis_size("core")


def seq_index():
    return lax.axis_index("sz") * lax.axis_size("core") + lax.axis_index("core")


def shifted(block, distance):
    count = seq_size()
    devices = range(count)
    route = [(i - distance, i) for i in devices if i - distance in devices]
    return lax.ppermute(block, SEQ, route)


def rope_tables(positions):
    pairs = HD // 2
    index = jnp.arange(pairs)
    inv_freq = jnp.exp(index.astype(jnp.float32) * (-2.0 * math.log(rope_base) / HD))
    temporal = HD // 8
    which = jnp.where(index >= pairs - temporal, 0, jnp.where(index % 2 == 0, 1, 2))
    places = positions.astype(jnp.float32)
    chosen = jnp.where((which == 0)[:, None], places[0][None, :], 0.0)
    chosen = chosen + jnp.where((which == 1)[:, None], places[1][None, :], 0.0)
    chosen = chosen + jnp.where((which == 2)[:, None], places[2][None, :], 0.0)
    angle = chosen.T * inv_freq[None, :]
    return (jnp.cos(angle), jnp.sin(angle))


def rotate(block, cosine, sine, sign):
    half = HD // 2
    first = block[..., :half]
    second = block[..., half:]
    cos_part = cosine[:, None, :]
    sin_part = sine[:, None, :] * sign
    return jnp.concatenate(
        [first * cos_part - second * sin_part, second * cos_part + first * sin_part], axis=-1
    )


def allowed_mask(shard, doc_query, doc_key, mask_rows):
    length = doc_query.shape[0]
    width = doc_key.shape[0]
    query_pos = shard * length + jnp.arange(length, dtype=jnp.int32)
    key_pos = (shard - REACH) * length + jnp.arange(width, dtype=jnp.int32)
    near = jnp.repeat(jnp.repeat(mask_rows, BLK, axis=0), BLK, axis=1) > 0
    same_block = query_pos[:, None] // BLK == key_pos[None, :] // BLK
    return (
        (doc_query[:, None] == doc_key[None, :])
        & (key_pos[None, :] <= query_pos[:, None])
        & (key_pos[None, :] >= 0)
        & (near | same_block)
    )


def attend(query, key_win, value_win, allowed, grad_out):
    scale = HD ** (-0.5)
    contract = (((1,), (1,)), ((), ()))
    columns = (((0,), (0,)), ((), ()))
    scores = lax.dot_general(query, key_win, contract, preferred_element_type=jnp.float32) * scale
    scores = jnp.where(allowed, scores, -1e30)
    top = jnp.max(scores, axis=1, keepdims=True)
    expo = jnp.exp(scores - top)
    weights = (expo / jnp.sum(expo, axis=1, keepdims=True)).astype(jnp.bfloat16)
    output = jnp.dot(weights, value_win, preferred_element_type=jnp.float32).astype(jnp.bfloat16)
    delta = jnp.sum(
        grad_out.astype(jnp.float32) * output.astype(jnp.float32), axis=1, keepdims=True
    )
    dprob = lax.dot_general(grad_out, value_win, contract, preferred_element_type=jnp.float32)
    dscore = (weights.astype(jnp.float32) * (dprob - delta)).astype(jnp.bfloat16)
    dquery = jnp.dot(dscore, key_win, preferred_element_type=jnp.float32) * scale
    dkey = lax.dot_general(dscore, query, columns, preferred_element_type=jnp.float32) * scale
    dvalue = lax.dot_general(weights, grad_out, columns, preferred_element_type=jnp.float32)
    return (output, dquery, dkey, dvalue)


def gather_window(packed):
    one = jnp.concatenate([shifted(packed, 1), packed], axis=0)
    two = jnp.concatenate([shifted(one, 2), one], axis=0)
    four = jnp.concatenate([shifted(two, 4), two], axis=0)
    far = shifted(one, 8)
    return jnp.concatenate([far, four], axis=0)


def return_window(pieces):
    far = shifted(pieces[:2].astype(jnp.bfloat16), -8).astype(jnp.float32)
    four = pieces[2:]
    two = four[4:] + shifted(four[:4].astype(jnp.bfloat16), -4).astype(jnp.float32)
    one = two[2:] + shifted(two[:2].astype(jnp.bfloat16), -2).astype(jnp.float32) + far
    return one[1] + shifted(one[:1].astype(jnp.bfloat16), -1).astype(jnp.float32)[0]


def per_device(queries, keys, values, out_weight, out_grad, doc_ids, block_mask, positions):
    length = queries.shape[0]
    groups = keys.shape[1] // HD
    heads = queries.shape[1] // HD
    per_group = heads // groups
    n_sz = lax.axis_size("sz")
    n_core = lax.axis_size("core")
    shard = seq_index()
    cosine, sine = rope_tables(positions)
    q_rot = (
        rotate(queries.astype(jnp.float32).reshape(length, heads, HD), cosine, sine, 1.0)
        .astype(jnp.bfloat16)
        .reshape(length, heads * HD)
    )
    k_rot = (
        rotate(keys.astype(jnp.float32).reshape(length, groups, HD), cosine, sine, 1.0)
        .astype(jnp.bfloat16)
        .reshape(length, groups * HD)
    )
    col_w = out_weight.shape[1]
    w_cols = lax.all_gather(out_weight, "sz", axis=1, tiled=True)
    w_cols = lax.all_gather(w_cols, "core", axis=1, tiled=True)
    og_perm = (
        out_grad.reshape(length, n_sz, n_core, col_w)
        .transpose(0, 2, 1, 3)
        .reshape(length, n_sz * n_core * col_w)
    )
    contract = (((1,), (1,)), ((), ()))
    hg_part = lax.dot_general(og_perm, w_cols, contract, preferred_element_type=jnp.float32)
    head_grad = lax.psum_scatter(
        hg_part.astype(jnp.bfloat16), "kv", scatter_dimension=1, tiled=True
    )
    width = keys.shape[1]
    doc_row = jnp.zeros((1, 2 * width), jnp.bfloat16).at[0, :length].set(
        doc_ids.astype(jnp.bfloat16)
    )
    packed = jnp.concatenate(
        [jnp.concatenate([k_rot, values], axis=1), doc_row], axis=0
    )[None]
    win = gather_window(packed)
    key_win = win[:, :length, :width].reshape(-1, width)
    value_win = win[:, :length, width:].reshape(-1, width)
    doc_win = win[:, length, :length].reshape(-1).astype(jnp.int32)
    blocks_dev = length // BLK
    mask_pad = jnp.pad(block_mask, ((0, 0), (REACH * blocks_dev, 0)))
    mask_rows = lax.dynamic_slice_in_dim(mask_pad, shard * blocks_dev, (REACH + 1) * blocks_dev, 1)
    allowed = allowed_mask(shard, doc_ids, doc_win, mask_rows)
    window = key_win.shape[0]
    outputs = []
    dqueries = []
    dkey_sum = jnp.zeros((window, HD), jnp.float32)
    dvalue_sum = jnp.zeros((window, HD), jnp.float32)
    for inner in range(per_group):
        output, dquery, dkey, dvalue = attend(
            q_rot[:, inner * HD : (inner + 1) * HD],
            key_win,
            value_win,
            allowed,
            head_grad[:, inner * HD : (inner + 1) * HD],
        )
        outputs.append(output)
        dqueries.append(dquery)
        dkey_sum = dkey_sum + dkey
        dvalue_sum = dvalue_sum + dvalue
    attn = jnp.concatenate(outputs, axis=1)
    dq_rot = jnp.stack(dqueries, axis=1)
    attn_all = lax.all_gather(attn, "kv", axis=1, tiled=True)
    kv_count = lax.axis_size("kv")
    rows = attn.shape[1]
    parts = jnp.einsum(
        "tgr,grc->gtc",
        attn_all.reshape(length, kv_count, rows),
        w_cols.reshape(kv_count, rows, -1),
        preferred_element_type=jnp.float32,
    ).astype(jnp.bfloat16)
    parts = lax.optimization_barrier(parts)
    out_perm = jnp.sum(parts.astype(jnp.float32), axis=0).astype(jnp.bfloat16)
    layer_out = (
        out_perm.reshape(length, n_core, n_sz, col_w)
        .transpose(0, 2, 1, 3)
        .reshape(length, n_sz * n_core * col_w)
    )
    dkv = jnp.concatenate([dkey_sum, dvalue_sum], axis=1).reshape(REACH + 1, length, 2 * HD)
    dkv_total = return_window(dkv)
    dk_total = dkv_total[:, :HD]
    dv_total = dkv_total[:, HD:]
    query_grad = rotate(dq_rot, cosine, sine, -1.0).astype(jnp.bfloat16).reshape(length, heads * HD)
    key_grad = (
        rotate(dk_total.reshape(length, groups, HD), cosine, sine, -1.0)
        .astype(jnp.bfloat16)
        .reshape(length, groups * HD)
    )
    value_grad = dv_total.astype(jnp.bfloat16)
    return (layer_out, query_grad, key_grad, value_grad)


def solution(mesh):
    n_seq, n_kv = mesh.devices.shape
    cores = 2 if n_seq % 2 == 0 else 1
    grid = Mesh(mesh.devices.reshape(n_seq // cores, cores, n_kv), ("sz", "core", "kv"))
    in_specs = (
        P(SEQ, "kv"),
        P(SEQ, "kv"),
        P(SEQ, "kv"),
        P(None, ("kv",) + SEQ),
        P(SEQ, "kv"),
        P(SEQ),
        P(SEQ, None),
        P(None, SEQ),
    )
    out_specs = (P(SEQ, "kv"), P(SEQ, "kv"), P(SEQ, "kv"), P(SEQ, "kv"))
    return jax.shard_map(
        per_device, mesh=grid, in_specs=in_specs, out_specs=out_specs, check_vma=False
    )
```

```python
import math

import jax
import jax.numpy as jnp
from jax import lax
from jax.sharding import Mesh
from jax.sharding import PartitionSpec as P

HD = 128
BLK = 128
REACH = 9

SEQ = ("sz", "core")

rope_base = 1000000.0


def seq_size():
    return lax.axis_size("sz") * lax.axis_size("core")


def seq_index():
    return lax.axis_index("sz") * lax.axis_size("core") + lax.axis_index("core")


def shifted(block, distance):
    count = seq_size()
    devices = range(count)
    route = [(i - distance, i) for i in devices if i - distance in devices]
    return lax.ppermute(block, SEQ, route)


def rope_tables(positions):
    pairs = HD // 2
    index = jnp.arange(pairs)
    inv_freq = jnp.exp(index.astype(jnp.float32) * (-2.0 * math.log(rope_base) / HD))
    temporal = HD // 8
    which = jnp.where(index >= pairs - temporal, 0, jnp.where(index % 2 == 0, 1, 2))
    places = positions.astype(jnp.float32)
    chosen = jnp.where((which == 0)[:, None], places[0][None, :], 0.0)
    chosen = chosen + jnp.where((which == 1)[:, None], places[1][None, :], 0.0)
    chosen = chosen + jnp.where((which == 2)[:, None], places[2][None, :], 0.0)
    angle = chosen.T * inv_freq[None, :]
    return (jnp.cos(angle), jnp.sin(angle))


def rotate(block, cosine, sine, sign):
    half = HD // 2
    first = block[..., :half]
    second = block[..., half:]
    cos_part = cosine[:, None, :]
    sin_part = sine[:, None, :] * sign
    return jnp.concatenate(
        [first * cos_part - second * sin_part, second * cos_part + first * sin_part], axis=-1
    )


def allowed_mask(shard, doc_query, doc_key, mask_rows):
    length = doc_query.shape[0]
    width = doc_key.shape[0]
    query_pos = shard * length + jnp.arange(length, dtype=jnp.int32)
    key_pos = (shard - REACH) * length + jnp.arange(width, dtype=jnp.int32)
    near = jnp.repeat(jnp.repeat(mask_rows, BLK, axis=0), BLK, axis=1) > 0
    same_block = query_pos[:, None] // BLK == key_pos[None, :] // BLK
    return (
        (doc_query[:, None] == doc_key[None, :])
        & (key_pos[None, :] <= query_pos[:, None])
        & (key_pos[None, :] >= 0)
        & (near | same_block)
    )


def attend(query, key_win, value_win, allowed, grad_out):
    scale = HD ** (-0.5)
    contract = (((1,), (1,)), ((), ()))
    columns = (((0,), (0,)), ((), ()))
    scores = lax.dot_general(query, key_win, contract, preferred_element_type=jnp.float32) * scale
    scores = jnp.where(allowed, scores, -1e30)
    top = jnp.max(scores, axis=1, keepdims=True)
    expo = jnp.exp(scores - top)
    weights = (expo / jnp.sum(expo, axis=1, keepdims=True)).astype(jnp.bfloat16)
    output = jnp.dot(weights, value_win, preferred_element_type=jnp.float32).astype(jnp.bfloat16)
    delta = jnp.sum(
        grad_out.astype(jnp.float32) * output.astype(jnp.float32), axis=1, keepdims=True
    )
    dprob = lax.dot_general(grad_out, value_win, contract, preferred_element_type=jnp.float32)
    dscore = (weights.astype(jnp.float32) * (dprob - delta)).astype(jnp.bfloat16)
    dquery = jnp.dot(dscore, key_win, preferred_element_type=jnp.float32) * scale
    dkey = lax.dot_general(dscore, query, columns, preferred_element_type=jnp.float32) * scale
    dvalue = lax.dot_general(weights, grad_out, columns, preferred_element_type=jnp.float32)
    return (output, dquery, dkey, dvalue)


def gather_window(packed):
    one = jnp.concatenate([shifted(packed, 1), packed], axis=0)
    two = jnp.concatenate([shifted(one, 2), one], axis=0)
    four = jnp.concatenate([shifted(two, 4), two], axis=0)
    far = shifted(one, 8)
    return jnp.concatenate([far, four], axis=0)


def return_window(pieces):
    far = shifted(pieces[:2].astype(jnp.bfloat16), -8).astype(jnp.float32)
    four = pieces[2:]
    two = four[4:] + shifted(four[:4].astype(jnp.bfloat16), -4).astype(jnp.float32)
    one = two[2:] + shifted(two[:2].astype(jnp.bfloat16), -2).astype(jnp.float32) + far
    return one[1] + shifted(one[:1].astype(jnp.bfloat16), -1).astype(jnp.float32)[0]


def per_device(queries, keys, values, out_weight, out_grad, doc_ids, block_mask, positions):
    length = queries.shape[0]
    groups = keys.shape[1] // HD
    heads = queries.shape[1] // HD
    per_group = heads // groups
    n_sz = lax.axis_size("sz")
    n_core = lax.axis_size("core")
    shard = seq_index()
    cosine, sine = rope_tables(positions)
    q_rot = (
        rotate(queries.astype(jnp.float32).reshape(length, heads, HD), cosine, sine, 1.0)
        .astype(jnp.bfloat16)
        .reshape(length, heads * HD)
    )
    k_rot = (
        rotate(keys.astype(jnp.float32).reshape(length, groups, HD), cosine, sine, 1.0)
        .astype(jnp.bfloat16)
        .reshape(length, groups * HD)
    )
    w_cols = lax.all_gather(out_weight, SEQ, axis=1, tiled=True)
    og_perm = out_grad
    contract = (((1,), (1,)), ((), ()))
    hg_part = lax.dot_general(og_perm, w_cols, contract, preferred_element_type=jnp.float32)
    head_grad = lax.psum_scatter(
        hg_part.astype(jnp.bfloat16), "kv", scatter_dimension=1, tiled=True
    )
    width = keys.shape[1]
    doc_row = jnp.zeros((1, 2 * width), jnp.bfloat16).at[0, :length].set(
        doc_ids.astype(jnp.bfloat16)
    )
    packed = jnp.concatenate(
        [jnp.concatenate([k_rot, values], axis=1), doc_row], axis=0
    )[None]
    win = gather_window(packed)
    key_win = win[:, :length, :width].reshape(-1, width)
    value_win = win[:, :length, width:].reshape(-1, width)
    doc_win = win[:, length, :length].reshape(-1).astype(jnp.int32)
    blocks_dev = length // BLK
    mask_pad = jnp.pad(block_mask, ((0, 0), (REACH * blocks_dev, 0)))
    mask_rows = lax.dynamic_slice_in_dim(mask_pad, shard * blocks_dev, (REACH + 1) * blocks_dev, 1)
    allowed = allowed_mask(shard, doc_ids, doc_win, mask_rows)
    window = key_win.shape[0]
    outputs = []
    dqueries = []
    dkey_sum = jnp.zeros((window, HD), jnp.float32)
    dvalue_sum = jnp.zeros((window, HD), jnp.float32)
    for inner in range(per_group):
        output, dquery, dkey, dvalue = attend(
            q_rot[:, inner * HD : (inner + 1) * HD],
            key_win,
            value_win,
            allowed,
            head_grad[:, inner * HD : (inner + 1) * HD],
        )
        outputs.append(output)
        dqueries.append(dquery)
        dkey_sum = dkey_sum + dkey
        dvalue_sum = dvalue_sum + dvalue
    attn = jnp.concatenate(outputs, axis=1)
    dq_rot = jnp.stack(dqueries, axis=1)
    kv_count = lax.axis_size("kv")
    kv_me = lax.axis_index("kv")
    rows = attn.shape[1]
    total = None
    for step in range(kv_count):
        if step == 0:
            piece = attn
        else:
            route = [(i, (i + step) % kv_count) for i in range(kv_count)]
            piece = lax.ppermute(attn, "kv", route)
        src = (kv_me - step) % kv_count
        w_rows = lax.dynamic_slice_in_dim(w_cols, src * rows, rows, 0)
        part = jnp.dot(piece, w_rows, preferred_element_type=jnp.float32).astype(jnp.bfloat16)
        part = lax.optimization_barrier(part)
        total = part.astype(jnp.float32) if total is None else total + part.astype(jnp.float32)
    layer_out = total.astype(jnp.bfloat16)
    dkv = jnp.concatenate([dkey_sum, dvalue_sum], axis=1).reshape(REACH + 1, length, 2 * HD)
    dkv_total = return_window(dkv)
    dk_total = dkv_total[:, :HD]
    dv_total = dkv_total[:, HD:]
    query_grad = rotate(dq_rot, cosine, sine, -1.0).astype(jnp.bfloat16).reshape(length, heads * HD)
    key_grad = (
        rotate(dk_total.reshape(length, groups, HD), cosine, sine, -1.0)
        .astype(jnp.bfloat16)
        .reshape(length, groups * HD)
    )
    value_grad = dv_total.astype(jnp.bfloat16)
    return (layer_out, query_grad, key_grad, value_grad)


def solution(mesh):
    n_seq, n_kv = mesh.devices.shape
    cores = 2 if n_seq % 2 == 0 else 1
    grid = Mesh(mesh.devices.reshape(n_seq // cores, cores, n_kv), ("sz", "core", "kv"))
    in_specs = (
        P(SEQ, "kv"),
        P(SEQ, "kv"),
        P(SEQ, "kv"),
        P(None, ("kv",) + SEQ),
        P(SEQ, "kv"),
        P(SEQ),
        P(SEQ, None),
        P(None, SEQ),
    )
    out_specs = (P(SEQ, "kv"), P(SEQ, "kv"), P(SEQ, "kv"), P(SEQ, "kv"))
    return jax.shard_map(
        per_device, mesh=grid, in_specs=in_specs, out_specs=out_specs, check_vma=False
    )
```

```python
import math

import jax
import jax.numpy as jnp
from jax import lax
from jax.sharding import Mesh
from jax.sharding import PartitionSpec as P

HD = 128
BLK = 128
REACH = 9

SEQ = ("sz", "core")

rope_base = 1000000.0


def seq_size():
    return lax.axis_size("sz") * lax.axis_size("core")


def seq_index():
    return lax.axis_index("sz") * lax.axis_size("core") + lax.axis_index("core")


def shifted(block, distance):
    count = seq_size()
    devices = range(count)
    route = [(i - distance, i) for i in devices if i - distance in devices]
    return lax.ppermute(block, SEQ, route)


def rope_tables(positions):
    pairs = HD // 2
    index = jnp.arange(pairs)
    inv_freq = jnp.exp(index.astype(jnp.float32) * (-2.0 * math.log(rope_base) / HD))
    temporal = HD // 8
    which = jnp.where(index >= pairs - temporal, 0, jnp.where(index % 2 == 0, 1, 2))
    places = positions.astype(jnp.float32)
    chosen = jnp.where((which == 0)[:, None], places[0][None, :], 0.0)
    chosen = chosen + jnp.where((which == 1)[:, None], places[1][None, :], 0.0)
    chosen = chosen + jnp.where((which == 2)[:, None], places[2][None, :], 0.0)
    angle = chosen.T * inv_freq[None, :]
    return (jnp.cos(angle), jnp.sin(angle))


def rotate(block, cosine, sine, sign):
    half = HD // 2
    first = block[..., :half]
    second = block[..., half:]
    cos_part = cosine[:, None, :]
    sin_part = sine[:, None, :] * sign
    return jnp.concatenate(
        [first * cos_part - second * sin_part, second * cos_part + first * sin_part], axis=-1
    )


def allowed_mask(shard, doc_query, doc_key, mask_rows):
    length = doc_query.shape[0]
    width = doc_key.shape[0]
    query_pos = shard * length + jnp.arange(length, dtype=jnp.int32)
    key_pos = (shard - REACH) * length + jnp.arange(width, dtype=jnp.int32)
    near = jnp.repeat(jnp.repeat(mask_rows, BLK, axis=0), BLK, axis=1) > 0
    same_block = query_pos[:, None] // BLK == key_pos[None, :] // BLK
    return (
        (doc_query[:, None] == doc_key[None, :])
        & (key_pos[None, :] <= query_pos[:, None])
        & (key_pos[None, :] >= 0)
        & (near | same_block)
    )


def attend(query, key_win, value_win, allowed, grad_out):
    scale = HD ** (-0.5)
    contract = (((1,), (1,)), ((), ()))
    columns = (((0,), (0,)), ((), ()))
    scores = lax.dot_general(query, key_win, contract, preferred_element_type=jnp.float32) * scale
    scores = jnp.where(allowed, scores, -1e30)
    top = jnp.max(scores, axis=1, keepdims=True)
    expo = jnp.exp(scores - top)
    weights = (expo / jnp.sum(expo, axis=1, keepdims=True)).astype(jnp.bfloat16)
    output = jnp.dot(weights, value_win, preferred_element_type=jnp.float32).astype(jnp.bfloat16)
    delta = jnp.sum(
        grad_out.astype(jnp.float32) * output.astype(jnp.float32), axis=1, keepdims=True
    )
    dprob = lax.dot_general(grad_out, value_win, contract, preferred_element_type=jnp.float32)
    dscore = (weights.astype(jnp.float32) * (dprob - delta)).astype(jnp.bfloat16)
    dquery = jnp.dot(dscore, key_win, preferred_element_type=jnp.float32) * scale
    dkey = lax.dot_general(dscore, query, columns, preferred_element_type=jnp.float32) * scale
    dvalue = lax.dot_general(weights, grad_out, columns, preferred_element_type=jnp.float32)
    return (output, dquery, dkey, dvalue)


def gather_window(packed):
    one = jnp.concatenate([shifted(packed, 1), packed], axis=0)
    two = jnp.concatenate([shifted(one, 2), one], axis=0)
    four = jnp.concatenate([shifted(two, 4), two], axis=0)
    far = shifted(one, 8)
    return jnp.concatenate([far, four], axis=0)


def return_window(pieces):
    far = shifted(pieces[:2].astype(jnp.bfloat16), -8).astype(jnp.float32)
    four = pieces[2:]
    two = four[4:] + shifted(four[:4].astype(jnp.bfloat16), -4).astype(jnp.float32)
    one = two[2:] + shifted(two[:2].astype(jnp.bfloat16), -2).astype(jnp.float32) + far
    return one[1] + shifted(one[:1].astype(jnp.bfloat16), -1).astype(jnp.float32)[0]


def per_device(queries, keys, values, out_weight, out_grad, doc_ids, block_mask, positions):
    length = queries.shape[0]
    groups = keys.shape[1] // HD
    heads = queries.shape[1] // HD
    per_group = heads // groups
    n_sz = lax.axis_size("sz")
    n_core = lax.axis_size("core")
    shard = seq_index()
    cosine, sine = rope_tables(positions)
    q_rot = (
        rotate(queries.astype(jnp.float32).reshape(length, heads, HD), cosine, sine, 1.0)
        .astype(jnp.bfloat16)
        .reshape(length, heads * HD)
    )
    k_rot = (
        rotate(keys.astype(jnp.float32).reshape(length, groups, HD), cosine, sine, 1.0)
        .astype(jnp.bfloat16)
        .reshape(length, groups * HD)
    )
    kv_count = lax.axis_size("kv")
    kv_me = lax.axis_index("kv")
    rows = queries.shape[1]
    order = list(range(1, kv_count)) + [0]
    chunk = 2 if kv_count % 2 == 0 else 1
    w_parts = {}
    for c in range(0, kv_count, chunk):
        steps = order[c : c + chunk]
        local = jnp.concatenate(
            [
                lax.dynamic_slice_in_dim(out_weight, ((kv_me + j) % kv_count) * rows, rows, 0)
                for j in steps
            ],
            axis=0,
        )
        gathered = lax.all_gather(local, SEQ, axis=1, tiled=True)
        for i, j in enumerate(steps):
            w_parts[j] = gathered[i * rows : (i + 1) * rows]
    contract = (((1,), (1,)), ((), ()))
    hg_sum = None
    for j in order:
        hg_j = lax.dot_general(
            out_grad, w_parts[j], contract, preferred_element_type=jnp.float32
        ).astype(jnp.bfloat16)
        if j != 0:
            hg_j = lax.ppermute(hg_j, "kv", [(i, (i + j) % kv_count) for i in range(kv_count)])
        hg_sum = hg_j.astype(jnp.float32) if hg_sum is None else hg_sum + hg_j.astype(jnp.float32)
    head_grad = hg_sum.astype(jnp.bfloat16)
    width = keys.shape[1]
    doc_row = jnp.zeros((1, 2 * width), jnp.bfloat16).at[0, :length].set(
        doc_ids.astype(jnp.bfloat16)
    )
    packed = jnp.concatenate(
        [jnp.concatenate([k_rot, values], axis=1), doc_row], axis=0
    )[None]
    win = gather_window(packed)
    key_win = win[:, :length, :width].reshape(-1, width)
    value_win = win[:, :length, width:].reshape(-1, width)
    doc_win = win[:, length, :length].reshape(-1).astype(jnp.int32)
    blocks_dev = length // BLK
    mask_pad = jnp.pad(block_mask, ((0, 0), (REACH * blocks_dev, 0)))
    mask_rows = lax.dynamic_slice_in_dim(mask_pad, shard * blocks_dev, (REACH + 1) * blocks_dev, 1)
    allowed = allowed_mask(shard, doc_ids, doc_win, mask_rows)
    window = key_win.shape[0]
    outputs = []
    dqueries = []
    dkey_sum = jnp.zeros((window, HD), jnp.float32)
    dvalue_sum = jnp.zeros((window, HD), jnp.float32)
    for inner in range(per_group):
        output, dquery, dkey, dvalue = attend(
            q_rot[:, inner * HD : (inner + 1) * HD],
            key_win,
            value_win,
            allowed,
            head_grad[:, inner * HD : (inner + 1) * HD],
        )
        outputs.append(output)
        dqueries.append(dquery)
        dkey_sum = dkey_sum + dkey
        dvalue_sum = dvalue_sum + dvalue
    attn = jnp.concatenate(outputs, axis=1)
    dq_rot = jnp.stack(dqueries, axis=1)
    total = None
    for j in order:
        piece = attn
        if j != 0:
            piece = lax.ppermute(attn, "kv", [(i, (i - j) % kv_count) for i in range(kv_count)])
        part = jnp.dot(piece, w_parts[j], preferred_element_type=jnp.float32).astype(jnp.bfloat16)
        part = lax.optimization_barrier(part)
        total = part.astype(jnp.float32) if total is None else total + part.astype(jnp.float32)
    layer_out = total.astype(jnp.bfloat16)
    dkv = jnp.concatenate([dkey_sum, dvalue_sum], axis=1).reshape(REACH + 1, length, 2 * HD)
    dkv_total = return_window(dkv)
    dk_total = dkv_total[:, :HD]
    dv_total = dkv_total[:, HD:]
    query_grad = rotate(dq_rot, cosine, sine, -1.0).astype(jnp.bfloat16).reshape(length, heads * HD)
    key_grad = (
        rotate(dk_total.reshape(length, groups, HD), cosine, sine, -1.0)
        .astype(jnp.bfloat16)
        .reshape(length, groups * HD)
    )
    value_grad = dv_total.astype(jnp.bfloat16)
    return (layer_out, query_grad, key_grad, value_grad)


def solution(mesh):
    n_seq, n_kv = mesh.devices.shape
    cores = 2 if n_seq % 2 == 0 else 1
    grid = Mesh(mesh.devices.reshape(n_seq // cores, cores, n_kv), ("sz", "core", "kv"))
    in_specs = (
        P(SEQ, "kv"),
        P(SEQ, "kv"),
        P(SEQ, "kv"),
        P(None, ("kv",) + SEQ),
        P(SEQ, "kv"),
        P(SEQ),
        P(SEQ, None),
        P(None, SEQ),
    )
    out_specs = (P(SEQ, "kv"), P(SEQ, "kv"), P(SEQ, "kv"), P(SEQ, "kv"))
    return jax.shard_map(
        per_device, mesh=grid, in_specs=in_specs, out_specs=out_specs, check_vma=False
    )
```

```python
import math

import jax
import jax.numpy as jnp
from jax import lax
from jax.sharding import Mesh
from jax.sharding import PartitionSpec as P

HD = 128
BLK = 128
REACH = 9

SEQ = ("sz", "core")

rope_base = 1000000.0


def seq_size():
    return lax.axis_size("sz") * lax.axis_size("core")


def seq_index():
    return lax.axis_index("sz") * lax.axis_size("core") + lax.axis_index("core")


def shifted(block, distance):
    count = seq_size()
    devices = range(count)
    route = [(i - distance, i) for i in devices if i - distance in devices]
    return lax.ppermute(block, SEQ, route)


def rope_tables(positions):
    pairs = HD // 2
    index = jnp.arange(pairs)
    inv_freq = jnp.exp(index.astype(jnp.float32) * (-2.0 * math.log(rope_base) / HD))
    temporal = HD // 8
    which = jnp.where(index >= pairs - temporal, 0, jnp.where(index % 2 == 0, 1, 2))
    places = positions.astype(jnp.float32)
    chosen = jnp.where((which == 0)[:, None], places[0][None, :], 0.0)
    chosen = chosen + jnp.where((which == 1)[:, None], places[1][None, :], 0.0)
    chosen = chosen + jnp.where((which == 2)[:, None], places[2][None, :], 0.0)
    angle = chosen.T * inv_freq[None, :]
    return (jnp.cos(angle), jnp.sin(angle))


def rotate(block, cosine, sine, sign):
    half = HD // 2
    first = block[..., :half]
    second = block[..., half:]
    cos_part = cosine[:, None, :]
    sin_part = sine[:, None, :] * sign
    return jnp.concatenate(
        [first * cos_part - second * sin_part, second * cos_part + first * sin_part], axis=-1
    )


def allowed_mask(shard, doc_query, doc_key, mask_rows):
    length = doc_query.shape[0]
    width = doc_key.shape[0]
    query_pos = shard * length + jnp.arange(length, dtype=jnp.int32)
    key_pos = (shard - REACH) * length + jnp.arange(width, dtype=jnp.int32)
    near = jnp.repeat(jnp.repeat(mask_rows, BLK, axis=0), BLK, axis=1) > 0
    same_block = query_pos[:, None] // BLK == key_pos[None, :] // BLK
    return (
        (doc_query[:, None] == doc_key[None, :])
        & (key_pos[None, :] <= query_pos[:, None])
        & (key_pos[None, :] >= 0)
        & (near | same_block)
    )


def attend(query, key_win, value_win, allowed, grad_out):
    scale = HD ** (-0.5)
    contract = (((1,), (1,)), ((), ()))
    columns = (((0,), (0,)), ((), ()))
    scores = lax.dot_general(query, key_win, contract, preferred_element_type=jnp.float32) * scale
    scores = jnp.where(allowed, scores, -1e30)
    top = jnp.max(scores, axis=1, keepdims=True)
    expo = jnp.exp(scores - top)
    weights = (expo / jnp.sum(expo, axis=1, keepdims=True)).astype(jnp.bfloat16)
    output = jnp.dot(weights, value_win, preferred_element_type=jnp.float32).astype(jnp.bfloat16)
    delta = jnp.sum(
        grad_out.astype(jnp.float32) * output.astype(jnp.float32), axis=1, keepdims=True
    )
    dprob = lax.dot_general(grad_out, value_win, contract, preferred_element_type=jnp.float32)
    dscore = (weights.astype(jnp.float32) * (dprob - delta)).astype(jnp.bfloat16)
    dquery = jnp.dot(dscore, key_win, preferred_element_type=jnp.float32) * scale
    dkey = lax.dot_general(dscore, query, columns, preferred_element_type=jnp.float32) * scale
    dvalue = lax.dot_general(weights, grad_out, columns, preferred_element_type=jnp.float32)
    return (output, dquery, dkey, dvalue)


def gather_window(packed):
    one = jnp.concatenate([shifted(packed, 1), packed], axis=0)
    two = jnp.concatenate([shifted(one, 2), one], axis=0)
    four = jnp.concatenate([shifted(two, 4), two], axis=0)
    far = shifted(one, 8)
    return jnp.concatenate([far, four], axis=0)


def return_window(pieces):
    far = shifted(pieces[:2].astype(jnp.bfloat16), -8).astype(jnp.float32)
    four = pieces[2:]
    two = four[4:] + shifted(four[:4].astype(jnp.bfloat16), -4).astype(jnp.float32)
    one = two[2:] + shifted(two[:2].astype(jnp.bfloat16), -2).astype(jnp.float32) + far
    return one[1] + shifted(one[:1].astype(jnp.bfloat16), -1).astype(jnp.float32)[0]


def per_device(queries, keys, values, out_weight, out_grad, doc_ids, block_mask, positions):
    length = queries.shape[0]
    groups = keys.shape[1] // HD
    heads = queries.shape[1] // HD
    per_group = heads // groups
    n_sz = lax.axis_size("sz")
    n_core = lax.axis_size("core")
    shard = seq_index()
    cosine, sine = rope_tables(positions)
    q_rot = (
        rotate(queries.astype(jnp.float32).reshape(length, heads, HD), cosine, sine, 1.0)
        .astype(jnp.bfloat16)
        .reshape(length, heads * HD)
    )
    k_rot = (
        rotate(keys.astype(jnp.float32).reshape(length, groups, HD), cosine, sine, 1.0)
        .astype(jnp.bfloat16)
        .reshape(length, groups * HD)
    )
    kv_count = lax.axis_size("kv")
    kv_me = lax.axis_index("kv")
    col_w = out_weight.shape[1]
    n_seq = seq_size()
    pieces = lax.all_to_all(out_weight, "kv", split_axis=0, concat_axis=1, tiled=True)
    stripes = lax.all_gather(pieces, SEQ, axis=1, tiled=True)
    og_list = [out_grad.reshape(length, n_seq, col_w)]
    for j in range(1, kv_count):
        got = lax.ppermute(out_grad, "kv", [(i, (i - j) % kv_count) for i in range(kv_count)])
        og_list.append(got.reshape(length, n_seq, col_w))
    og_stack = jnp.stack(og_list, axis=2)
    og_perm = jnp.roll(og_stack, kv_me, axis=2).reshape(length, -1)
    contract = (((1,), (1,)), ((), ()))
    head_grad = lax.dot_general(
        og_perm, stripes, contract, preferred_element_type=jnp.float32
    ).astype(jnp.bfloat16)
    width = keys.shape[1]
    doc_row = jnp.zeros((1, 2 * width), jnp.bfloat16).at[0, :length].set(
        doc_ids.astype(jnp.bfloat16)
    )
    packed = jnp.concatenate(
        [jnp.concatenate([k_rot, values], axis=1), doc_row], axis=0
    )[None]
    win = gather_window(packed)
    key_win = win[:, :length, :width].reshape(-1, width)
    value_win = win[:, :length, width:].reshape(-1, width)
    doc_win = win[:, length, :length].reshape(-1).astype(jnp.int32)
    blocks_dev = length // BLK
    mask_pad = jnp.pad(block_mask, ((0, 0), (REACH * blocks_dev, 0)))
    mask_rows = lax.dynamic_slice_in_dim(mask_pad, shard * blocks_dev, (REACH + 1) * blocks_dev, 1)
    allowed = allowed_mask(shard, doc_ids, doc_win, mask_rows)
    window = key_win.shape[0]
    outputs = []
    dqueries = []
    dkey_sum = jnp.zeros((window, HD), jnp.float32)
    dvalue_sum = jnp.zeros((window, HD), jnp.float32)
    for inner in range(per_group):
        output, dquery, dkey, dvalue = attend(
            q_rot[:, inner * HD : (inner + 1) * HD],
            key_win,
            value_win,
            allowed,
            head_grad[:, inner * HD : (inner + 1) * HD],
        )
        outputs.append(output)
        dqueries.append(dquery)
        dkey_sum = dkey_sum + dkey
        dvalue_sum = dvalue_sum + dvalue
    attn = jnp.concatenate(outputs, axis=1)
    dq_rot = jnp.stack(dqueries, axis=1)
    lo_part = jnp.dot(attn, stripes, preferred_element_type=jnp.float32).astype(jnp.bfloat16)
    lo_part = lo_part.reshape(length, n_seq, kv_count, col_w)
    total = lax.dynamic_index_in_dim(lo_part, kv_me, 2, keepdims=False).astype(jnp.float32)
    for j in range(1, kv_count):
        dest = (kv_me + j) % kv_count
        piece = lax.dynamic_index_in_dim(lo_part, dest, 2, keepdims=False)
        got = lax.ppermute(piece, "kv", [(i, (i + j) % kv_count) for i in range(kv_count)])
        total = total + got.astype(jnp.float32)
    layer_out = total.reshape(length, n_seq * col_w).astype(jnp.bfloat16)
    dkv = jnp.concatenate([dkey_sum, dvalue_sum], axis=1).reshape(REACH + 1, length, 2 * HD)
    dkv_total = return_window(dkv)
    dk_total = dkv_total[:, :HD]
    dv_total = dkv_total[:, HD:]
    query_grad = rotate(dq_rot, cosine, sine, -1.0).astype(jnp.bfloat16).reshape(length, heads * HD)
    key_grad = (
        rotate(dk_total.reshape(length, groups, HD), cosine, sine, -1.0)
        .astype(jnp.bfloat16)
        .reshape(length, groups * HD)
    )
    value_grad = dv_total.astype(jnp.bfloat16)
    return (layer_out, query_grad, key_grad, value_grad)


def solution(mesh):
    n_seq, n_kv = mesh.devices.shape
    cores = 2 if n_seq % 2 == 0 else 1
    grid = Mesh(mesh.devices.reshape(n_seq // cores, cores, n_kv), ("sz", "core", "kv"))
    in_specs = (
        P(SEQ, "kv"),
        P(SEQ, "kv"),
        P(SEQ, "kv"),
        P(None, ("kv",) + SEQ),
        P(SEQ, "kv"),
        P(SEQ),
        P(SEQ, None),
        P(None, SEQ),
    )
    out_specs = (P(SEQ, "kv"), P(SEQ, "kv"), P(SEQ, "kv"), P(SEQ, "kv"))
    return jax.shard_map(
        per_device, mesh=grid, in_specs=in_specs, out_specs=out_specs, check_vma=False
    )
```

```python
import math

import jax
import jax.numpy as jnp
from jax import lax
from jax.sharding import Mesh
from jax.sharding import PartitionSpec as P

HD = 128
BLK = 128
REACH = 9

SEQ = ("sz", "core")

rope_base = 1000000.0


def seq_size():
    return lax.axis_size("sz") * lax.axis_size("core")


def seq_index():
    return lax.axis_index("sz") * lax.axis_size("core") + lax.axis_index("core")


def shifted(block, distance):
    count = seq_size()
    devices = range(count)
    route = [(i - distance, i) for i in devices if i - distance in devices]
    return lax.ppermute(block, SEQ, route)


def rope_tables(positions):
    pairs = HD // 2
    index = jnp.arange(pairs)
    inv_freq = jnp.exp(index.astype(jnp.float32) * (-2.0 * math.log(rope_base) / HD))
    temporal = HD // 8
    which = jnp.where(index >= pairs - temporal, 0, jnp.where(index % 2 == 0, 1, 2))
    places = positions.astype(jnp.float32)
    chosen = jnp.where((which == 0)[:, None], places[0][None, :], 0.0)
    chosen = chosen + jnp.where((which == 1)[:, None], places[1][None, :], 0.0)
    chosen = chosen + jnp.where((which == 2)[:, None], places[2][None, :], 0.0)
    angle = chosen.T * inv_freq[None, :]
    return (jnp.cos(angle), jnp.sin(angle))


def rotate(block, cosine, sine, sign):
    half = HD // 2
    first = block[..., :half]
    second = block[..., half:]
    cos_part = cosine[:, None, :]
    sin_part = sine[:, None, :] * sign
    return jnp.concatenate(
        [first * cos_part - second * sin_part, second * cos_part + first * sin_part], axis=-1
    )


def allowed_mask(shard, doc_query, doc_key, mask_rows):
    length = doc_query.shape[0]
    width = doc_key.shape[0]
    query_pos = shard * length + jnp.arange(length, dtype=jnp.int32)
    key_pos = (shard - REACH) * length + jnp.arange(width, dtype=jnp.int32)
    near = jnp.repeat(jnp.repeat(mask_rows, BLK, axis=0), BLK, axis=1) > 0
    same_block = query_pos[:, None] // BLK == key_pos[None, :] // BLK
    return (
        (doc_query[:, None] == doc_key[None, :])
        & (key_pos[None, :] <= query_pos[:, None])
        & (key_pos[None, :] >= 0)
        & (near | same_block)
    )


def attend(query, key_win, value_win, allowed, grad_out):
    scale = HD ** (-0.5)
    contract = (((1,), (1,)), ((), ()))
    columns = (((0,), (0,)), ((), ()))
    scores = lax.dot_general(query, key_win, contract, preferred_element_type=jnp.float32) * scale
    scores = jnp.where(allowed, scores, -1e30)
    top = jnp.max(scores, axis=1, keepdims=True)
    expo = jnp.exp(scores - top)
    weights = (expo / jnp.sum(expo, axis=1, keepdims=True)).astype(jnp.bfloat16)
    output = jnp.dot(weights, value_win, preferred_element_type=jnp.float32).astype(jnp.bfloat16)
    delta = jnp.sum(
        grad_out.astype(jnp.float32) * output.astype(jnp.float32), axis=1, keepdims=True
    )
    dprob = lax.dot_general(grad_out, value_win, contract, preferred_element_type=jnp.float32)
    dscore = (weights.astype(jnp.float32) * (dprob - delta)).astype(jnp.bfloat16)
    dquery = jnp.dot(dscore, key_win, preferred_element_type=jnp.float32) * scale
    dkey = lax.dot_general(dscore, query, columns, preferred_element_type=jnp.float32) * scale
    dvalue = lax.dot_general(weights, grad_out, columns, preferred_element_type=jnp.float32)
    return (output, dquery, dkey, dvalue)


def gather_window(packed):
    one = jnp.concatenate([shifted(packed, 1), packed], axis=0)
    two = jnp.concatenate([shifted(one, 2), one], axis=0)
    four = jnp.concatenate([shifted(two, 4), two], axis=0)
    far = shifted(one, 8)
    return jnp.concatenate([far, four], axis=0)


def return_window(pieces):
    far = shifted(pieces[:2].astype(jnp.bfloat16), -8).astype(jnp.float32)
    four = pieces[2:]
    two = four[4:] + shifted(four[:4].astype(jnp.bfloat16), -4).astype(jnp.float32)
    one = two[2:] + shifted(two[:2].astype(jnp.bfloat16), -2).astype(jnp.float32) + far
    return one[1] + shifted(one[:1].astype(jnp.bfloat16), -1).astype(jnp.float32)[0]


def per_device(queries, keys, values, out_weight, out_grad, doc_ids, block_mask, positions):
    length = queries.shape[0]
    groups = keys.shape[1] // HD
    heads = queries.shape[1] // HD
    per_group = heads // groups
    n_sz = lax.axis_size("sz")
    n_core = lax.axis_size("core")
    shard = seq_index()
    cosine, sine = rope_tables(positions)
    q_rot = (
        rotate(queries.astype(jnp.float32).reshape(length, heads, HD), cosine, sine, 1.0)
        .astype(jnp.bfloat16)
        .reshape(length, heads * HD)
    )
    k_rot = (
        rotate(keys.astype(jnp.float32).reshape(length, groups, HD), cosine, sine, 1.0)
        .astype(jnp.bfloat16)
        .reshape(length, groups * HD)
    )
    kv_count = lax.axis_size("kv")
    kv_me = lax.axis_index("kv")
    col_w = out_weight.shape[1]
    n_seq = seq_size()
    pieces = lax.all_to_all(out_weight, "kv", split_axis=0, concat_axis=1, tiled=True)
    stripes = lax.all_gather(pieces, SEQ, axis=1, tiled=True)
    og_list = [out_grad.reshape(length, n_seq, col_w)]
    for j in range(1, kv_count):
        got = lax.ppermute(out_grad, "kv", [(i, (i - j) % kv_count) for i in range(kv_count)])
        og_list.append(got.reshape(length, n_seq, col_w))
    og_stack = jnp.stack(og_list, axis=2)
    og_perm = jnp.roll(og_stack, kv_me, axis=2).reshape(length, -1)
    contract = (((1,), (1,)), ((), ()))
    head_grad = lax.dot_general(
        og_perm, stripes, contract, preferred_element_type=jnp.float32
    ).astype(jnp.bfloat16)
    width = keys.shape[1]
    doc_row = jnp.zeros((1, 2 * width), jnp.bfloat16).at[0, :length].set(
        doc_ids.astype(jnp.bfloat16)
    )
    packed = jnp.concatenate(
        [jnp.concatenate([k_rot, values], axis=1), doc_row], axis=0
    )[None]
    win = gather_window(packed)
    key_win = win[:, :length, :width].reshape(-1, width)
    value_win = win[:, :length, width:].reshape(-1, width)
    doc_win = win[:, length, :length].reshape(-1).astype(jnp.int32)
    blocks_dev = length // BLK
    mask_pad = jnp.pad(block_mask, ((0, 0), (REACH * blocks_dev, 0)))
    mask_rows = lax.dynamic_slice_in_dim(mask_pad, shard * blocks_dev, (REACH + 1) * blocks_dev, 1)
    allowed = allowed_mask(shard, doc_ids, doc_win, mask_rows)
    scale = HD ** (-0.5)
    q_grp = q_rot.reshape(length, per_group, HD)
    g_grp = head_grad.reshape(length, per_group, HD)
    scores = jnp.einsum("thd,ud->htu", q_grp, key_win, preferred_element_type=jnp.float32) * scale
    scores = jnp.where(allowed[None], scores, -1e30)
    top = jnp.max(scores, axis=2, keepdims=True)
    expo = jnp.exp(scores - top)
    weights = (expo / jnp.sum(expo, axis=2, keepdims=True)).astype(jnp.bfloat16)
    out_grp = jnp.einsum(
        "htu,ud->thd", weights, value_win, preferred_element_type=jnp.float32
    ).astype(jnp.bfloat16)
    delta = jnp.sum(g_grp.astype(jnp.float32) * out_grp.astype(jnp.float32), axis=2)
    dprob = jnp.einsum("thd,ud->htu", g_grp, value_win, preferred_element_type=jnp.float32)
    dscore = (weights.astype(jnp.float32) * (dprob - delta.T[:, :, None])).astype(jnp.bfloat16)
    dq_rot = jnp.einsum("htu,ud->thd", dscore, key_win, preferred_element_type=jnp.float32) * scale
    dkey_sum = jnp.einsum("htu,thd->ud", dscore, q_grp, preferred_element_type=jnp.float32) * scale
    dvalue_sum = jnp.einsum("htu,thd->ud", weights, g_grp, preferred_element_type=jnp.float32)
    attn = out_grp.reshape(length, per_group * HD)
    lo_part = jnp.dot(attn, stripes, preferred_element_type=jnp.float32).astype(jnp.bfloat16)
    lo_part = lo_part.reshape(length, n_seq, kv_count, col_w)
    total = lax.dynamic_index_in_dim(lo_part, kv_me, 2, keepdims=False).astype(jnp.float32)
    for j in range(1, kv_count):
        dest = (kv_me + j) % kv_count
        piece = lax.dynamic_index_in_dim(lo_part, dest, 2, keepdims=False)
        got = lax.ppermute(piece, "kv", [(i, (i + j) % kv_count) for i in range(kv_count)])
        total = total + got.astype(jnp.float32)
    layer_out = total.reshape(length, n_seq * col_w).astype(jnp.bfloat16)
    dkv = jnp.concatenate([dkey_sum, dvalue_sum], axis=1).reshape(REACH + 1, length, 2 * HD)
    dkv_total = return_window(dkv)
    dk_total = dkv_total[:, :HD]
    dv_total = dkv_total[:, HD:]
    query_grad = rotate(dq_rot, cosine, sine, -1.0).astype(jnp.bfloat16).reshape(length, heads * HD)
    key_grad = (
        rotate(dk_total.reshape(length, groups, HD), cosine, sine, -1.0)
        .astype(jnp.bfloat16)
        .reshape(length, groups * HD)
    )
    value_grad = dv_total.astype(jnp.bfloat16)
    return (layer_out, query_grad, key_grad, value_grad)


def solution(mesh):
    n_seq, n_kv = mesh.devices.shape
    cores = 2 if n_seq % 2 == 0 else 1
    grid = Mesh(mesh.devices.reshape(n_seq // cores, cores, n_kv), ("sz", "core", "kv"))
    in_specs = (
        P(SEQ, "kv"),
        P(SEQ, "kv"),
        P(SEQ, "kv"),
        P(None, ("kv",) + SEQ),
        P(SEQ, "kv"),
        P(SEQ),
        P(SEQ, None),
        P(None, SEQ),
    )
    out_specs = (P(SEQ, "kv"), P(SEQ, "kv"), P(SEQ, "kv"), P(SEQ, "kv"))
    return jax.shard_map(
        per_device, mesh=grid, in_specs=in_specs, out_specs=out_specs, check_vma=False
    )
```

```python
import math

import jax
import jax.numpy as jnp
from jax import lax
from jax.sharding import Mesh
from jax.sharding import PartitionSpec as P

HD = 128
BLK = 128
REACH = 9

SEQ = ("sz", "core")

rope_base = 1000000.0


def seq_size():
    return lax.axis_size("sz") * lax.axis_size("core")


def seq_index():
    return lax.axis_index("sz") * lax.axis_size("core") + lax.axis_index("core")


def shifted(block, distance):
    count = seq_size()
    devices = range(count)
    route = [(i - distance, i) for i in devices if i - distance in devices]
    return lax.ppermute(block, SEQ, route)


def rope_tables(positions):
    pairs = HD // 2
    index = jnp.arange(pairs)
    inv_freq = jnp.exp(index.astype(jnp.float32) * (-2.0 * math.log(rope_base) / HD))
    temporal = HD // 8
    which = jnp.where(index >= pairs - temporal, 0, jnp.where(index % 2 == 0, 1, 2))
    places = positions.astype(jnp.float32)
    chosen = jnp.where((which == 0)[:, None], places[0][None, :], 0.0)
    chosen = chosen + jnp.where((which == 1)[:, None], places[1][None, :], 0.0)
    chosen = chosen + jnp.where((which == 2)[:, None], places[2][None, :], 0.0)
    angle = chosen.T * inv_freq[None, :]
    return (jnp.cos(angle), jnp.sin(angle))


def rotate(block, cosine, sine, sign):
    half = HD // 2
    first = block[..., :half]
    second = block[..., half:]
    cos_part = cosine[:, None, :]
    sin_part = sine[:, None, :] * sign
    return jnp.concatenate(
        [first * cos_part - second * sin_part, second * cos_part + first * sin_part], axis=-1
    )


def allowed_mask(shard, doc_query, doc_key, mask_rows):
    length = doc_query.shape[0]
    width = doc_key.shape[0]
    query_pos = shard * length + jnp.arange(length, dtype=jnp.int32)
    key_pos = (shard - REACH) * length + jnp.arange(width, dtype=jnp.int32)
    near = jnp.repeat(jnp.repeat(mask_rows, BLK, axis=0), BLK, axis=1) > 0
    same_block = query_pos[:, None] // BLK == key_pos[None, :] // BLK
    return (
        (doc_query[:, None] == doc_key[None, :])
        & (key_pos[None, :] <= query_pos[:, None])
        & (key_pos[None, :] >= 0)
        & (near | same_block)
    )


def attend(query, key_win, value_win, allowed, grad_out):
    scale = HD ** (-0.5)
    contract = (((1,), (1,)), ((), ()))
    columns = (((0,), (0,)), ((), ()))
    scores = lax.dot_general(query, key_win, contract, preferred_element_type=jnp.float32) * scale
    scores = jnp.where(allowed, scores, -1e30)
    top = jnp.max(scores, axis=1, keepdims=True)
    expo = jnp.exp(scores - top)
    weights = (expo / jnp.sum(expo, axis=1, keepdims=True)).astype(jnp.bfloat16)
    output = jnp.dot(weights, value_win, preferred_element_type=jnp.float32).astype(jnp.bfloat16)
    delta = jnp.sum(
        grad_out.astype(jnp.float32) * output.astype(jnp.float32), axis=1, keepdims=True
    )
    dprob = lax.dot_general(grad_out, value_win, contract, preferred_element_type=jnp.float32)
    dscore = (weights.astype(jnp.float32) * (dprob - delta)).astype(jnp.bfloat16)
    dquery = jnp.dot(dscore, key_win, preferred_element_type=jnp.float32) * scale
    dkey = lax.dot_general(dscore, query, columns, preferred_element_type=jnp.float32) * scale
    dvalue = lax.dot_general(weights, grad_out, columns, preferred_element_type=jnp.float32)
    return (output, dquery, dkey, dvalue)


def gather_window(packed):
    one = jnp.concatenate([shifted(packed, 1), packed], axis=0)
    two = jnp.concatenate([shifted(one, 2), one], axis=0)
    four = jnp.concatenate([shifted(two, 4), two], axis=0)
    far = shifted(one, 8)
    return jnp.concatenate([far, four], axis=0)


def return_window(pieces):
    far = shifted(pieces[:2].astype(jnp.bfloat16), -8).astype(jnp.float32)
    four = pieces[2:]
    two = four[4:] + shifted(four[:4].astype(jnp.bfloat16), -4).astype(jnp.float32)
    one = two[2:] + shifted(two[:2].astype(jnp.bfloat16), -2).astype(jnp.float32) + far
    return one[1] + shifted(one[:1].astype(jnp.bfloat16), -1).astype(jnp.float32)[0]


def per_device(queries, keys, values, out_weight, out_grad, doc_ids, block_mask, positions):
    length = queries.shape[0]
    groups = keys.shape[1] // HD
    heads = queries.shape[1] // HD
    per_group = heads // groups
    n_sz = lax.axis_size("sz")
    n_core = lax.axis_size("core")
    shard = seq_index()
    cosine, sine = rope_tables(positions)
    q_rot = (
        rotate(queries.astype(jnp.float32).reshape(length, heads, HD), cosine, sine, 1.0)
        .astype(jnp.bfloat16)
        .reshape(length, heads * HD)
    )
    k_rot = (
        rotate(keys.astype(jnp.float32).reshape(length, groups, HD), cosine, sine, 1.0)
        .astype(jnp.bfloat16)
        .reshape(length, groups * HD)
    )
    kv_count = lax.axis_size("kv")
    kv_me = lax.axis_index("kv")
    col_w = out_weight.shape[1]
    n_seq = seq_size()
    pieces = lax.all_to_all(out_weight, "kv", split_axis=0, concat_axis=1, tiled=True)
    stripes = lax.all_gather(pieces, SEQ, axis=1, tiled=True)
    og_list = [out_grad.reshape(length, n_seq, col_w)]
    for j in range(1, kv_count):
        got = lax.ppermute(out_grad, "kv", [(i, (i - j) % kv_count) for i in range(kv_count)])
        og_list.append(got.reshape(length, n_seq, col_w))
    og_stack = jnp.stack(og_list, axis=2)
    og_perm = jnp.roll(og_stack, kv_me, axis=2).reshape(length, -1)
    contract = (((1,), (1,)), ((), ()))
    head_grad = lax.dot_general(
        og_perm, stripes, contract, preferred_element_type=jnp.float32
    ).astype(jnp.bfloat16)
    width = keys.shape[1]
    doc_row = jnp.zeros((1, 2 * width), jnp.bfloat16).at[0, :length].set(
        doc_ids.astype(jnp.bfloat16)
    )
    packed = jnp.concatenate(
        [jnp.concatenate([k_rot, values], axis=1), doc_row], axis=0
    )[None]
    win = gather_window(packed)
    key_win = win[:, :length, :width].reshape(-1, width)
    value_win = win[:, :length, width:].reshape(-1, width)
    doc_win = win[:, length, :length].reshape(-1).astype(jnp.int32)
    blocks_dev = length // BLK
    mask_pad = jnp.pad(block_mask, ((0, 0), (REACH * blocks_dev, 0)))
    mask_rows = lax.dynamic_slice_in_dim(mask_pad, shard * blocks_dev, (REACH + 1) * blocks_dev, 1)
    allowed = allowed_mask(shard, doc_ids, doc_win, mask_rows)
    scale = HD ** (-0.5)
    q_grp = q_rot.reshape(length, per_group, HD)
    g_grp = head_grad.reshape(length, per_group, HD)
    scores = jnp.einsum("thd,ud->htu", q_grp, key_win, preferred_element_type=jnp.float32) * scale
    scores = jnp.where(allowed[None], scores, -1e30)
    top = jnp.max(scores, axis=2, keepdims=True)
    expo = jnp.exp(scores - top)
    weights = (expo / jnp.sum(expo, axis=2, keepdims=True)).astype(jnp.bfloat16)
    out_grp = jnp.einsum(
        "htu,ud->thd", weights, value_win, preferred_element_type=jnp.float32
    ).astype(jnp.bfloat16)
    delta = jnp.sum(g_grp.astype(jnp.float32) * out_grp.astype(jnp.float32), axis=2)
    dprob = jnp.einsum("thd,ud->htu", g_grp, value_win, preferred_element_type=jnp.float32)
    dscore = (weights.astype(jnp.float32) * (dprob - delta.T[:, :, None])).astype(jnp.bfloat16)
    dq_rot = jnp.einsum("htu,ud->thd", dscore, key_win, preferred_element_type=jnp.float32) * scale
    dkey_sum = jnp.einsum("htu,thd->ud", dscore, q_grp, preferred_element_type=jnp.float32) * scale
    dvalue_sum = jnp.einsum("htu,thd->ud", weights, g_grp, preferred_element_type=jnp.float32)
    attn = out_grp.reshape(length, per_group * HD)
    dkv = jnp.concatenate([dkey_sum, dvalue_sum], axis=1).reshape(REACH + 1, length, 2 * HD)
    attn, dkv = lax.optimization_barrier((attn, dkv))
    lo_part = jnp.einsum(
        "tr,rskj->ktsj",
        attn,
        stripes.reshape(attn.shape[1], n_seq, kv_count, col_w),
        preferred_element_type=jnp.float32,
    ).astype(jnp.bfloat16)
    total = lax.dynamic_index_in_dim(lo_part, kv_me, 0, keepdims=False).astype(jnp.float32)
    for j in range(1, kv_count):
        dest = (kv_me + j) % kv_count
        piece = lax.dynamic_index_in_dim(lo_part, dest, 0, keepdims=False)
        got = lax.ppermute(piece, "kv", [(i, (i + j) % kv_count) for i in range(kv_count)])
        total = total + got.astype(jnp.float32)
    layer_out = total.reshape(length, n_seq * col_w).astype(jnp.bfloat16)
    dkv_total = return_window(dkv)
    dk_total = dkv_total[:, :HD]
    dv_total = dkv_total[:, HD:]
    query_grad = rotate(dq_rot, cosine, sine, -1.0).astype(jnp.bfloat16).reshape(length, heads * HD)
    key_grad = (
        rotate(dk_total.reshape(length, groups, HD), cosine, sine, -1.0)
        .astype(jnp.bfloat16)
        .reshape(length, groups * HD)
    )
    value_grad = dv_total.astype(jnp.bfloat16)
    return (layer_out, query_grad, key_grad, value_grad)


def solution(mesh):
    n_seq, n_kv = mesh.devices.shape
    cores = 2 if n_seq % 2 == 0 else 1
    grid = Mesh(mesh.devices.reshape(n_seq // cores, cores, n_kv), ("sz", "core", "kv"))
    in_specs = (
        P(SEQ, "kv"),
        P(SEQ, "kv"),
        P(SEQ, "kv"),
        P(None, ("kv",) + SEQ),
        P(SEQ, "kv"),
        P(SEQ),
        P(SEQ, None),
        P(None, SEQ),
    )
    out_specs = (P(SEQ, "kv"), P(SEQ, "kv"), P(SEQ, "kv"), P(SEQ, "kv"))
    return jax.shard_map(
        per_device, mesh=grid, in_specs=in_specs, out_specs=out_specs, check_vma=False
    )
```

```python
import math

import jax
import jax.numpy as jnp
from jax import lax
from jax.sharding import Mesh
from jax.sharding import PartitionSpec as P

HD = 128
BLK = 128
REACH = 9

SEQ = ("sz", "core")

rope_base = 1000000.0


def seq_size():
    return lax.axis_size("sz") * lax.axis_size("core")


def seq_index():
    return lax.axis_index("sz") * lax.axis_size("core") + lax.axis_index("core")


def shifted(block, distance):
    count = seq_size()
    devices = range(count)
    route = [(i - distance, i) for i in devices if i - distance in devices]
    return lax.ppermute(block, SEQ, route)


def rope_tables(positions):
    pairs = HD // 2
    index = jnp.arange(pairs)
    inv_freq = jnp.exp(index.astype(jnp.float32) * (-2.0 * math.log(rope_base) / HD))
    temporal = HD // 8
    which = jnp.where(index >= pairs - temporal, 0, jnp.where(index % 2 == 0, 1, 2))
    places = positions.astype(jnp.float32)
    chosen = jnp.where((which == 0)[:, None], places[0][None, :], 0.0)
    chosen = chosen + jnp.where((which == 1)[:, None], places[1][None, :], 0.0)
    chosen = chosen + jnp.where((which == 2)[:, None], places[2][None, :], 0.0)
    angle = chosen.T * inv_freq[None, :]
    return (jnp.cos(angle), jnp.sin(angle))


def rotate(block, cosine, sine, sign):
    half = HD // 2
    first = block[..., :half]
    second = block[..., half:]
    cos_part = cosine[:, None, :]
    sin_part = sine[:, None, :] * sign
    return jnp.concatenate(
        [first * cos_part - second * sin_part, second * cos_part + first * sin_part], axis=-1
    )


def allowed_mask(shard, doc_query, doc_key, mask_rows):
    length = doc_query.shape[0]
    width = doc_key.shape[0]
    query_pos = shard * length + jnp.arange(length, dtype=jnp.int32)
    key_pos = (shard - REACH) * length + jnp.arange(width, dtype=jnp.int32)
    near = jnp.repeat(jnp.repeat(mask_rows, BLK, axis=0), BLK, axis=1) > 0
    same_block = query_pos[:, None] // BLK == key_pos[None, :] // BLK
    return (
        (doc_query[:, None] == doc_key[None, :])
        & (key_pos[None, :] <= query_pos[:, None])
        & (key_pos[None, :] >= 0)
        & (near | same_block)
    )


def attend(query, key_win, value_win, allowed, grad_out):
    scale = HD ** (-0.5)
    contract = (((1,), (1,)), ((), ()))
    columns = (((0,), (0,)), ((), ()))
    scores = lax.dot_general(query, key_win, contract, preferred_element_type=jnp.float32) * scale
    scores = jnp.where(allowed, scores, -1e30)
    top = jnp.max(scores, axis=1, keepdims=True)
    expo = jnp.exp(scores - top)
    weights = (expo / jnp.sum(expo, axis=1, keepdims=True)).astype(jnp.bfloat16)
    output = jnp.dot(weights, value_win, preferred_element_type=jnp.float32).astype(jnp.bfloat16)
    delta = jnp.sum(
        grad_out.astype(jnp.float32) * output.astype(jnp.float32), axis=1, keepdims=True
    )
    dprob = lax.dot_general(grad_out, value_win, contract, preferred_element_type=jnp.float32)
    dscore = (weights.astype(jnp.float32) * (dprob - delta)).astype(jnp.bfloat16)
    dquery = jnp.dot(dscore, key_win, preferred_element_type=jnp.float32) * scale
    dkey = lax.dot_general(dscore, query, columns, preferred_element_type=jnp.float32) * scale
    dvalue = lax.dot_general(weights, grad_out, columns, preferred_element_type=jnp.float32)
    return (output, dquery, dkey, dvalue)


def gather_window(packed):
    one = jnp.concatenate([shifted(packed, 1), packed], axis=0)
    two = jnp.concatenate([shifted(one, 2), one], axis=0)
    four = jnp.concatenate([shifted(two, 4), two], axis=0)
    far = shifted(one, 8)
    return jnp.concatenate([far, four], axis=0)


def return_window(pieces):
    total = pieces[REACH]
    for reach in range(1, REACH + 1):
        back = shifted(pieces[REACH - reach].astype(jnp.bfloat16), -reach)
        total = total + back.astype(jnp.float32)
    return total


def per_device(queries, keys, values, out_weight, out_grad, doc_ids, block_mask, positions):
    length = queries.shape[0]
    groups = keys.shape[1] // HD
    heads = queries.shape[1] // HD
    per_group = heads // groups
    n_sz = lax.axis_size("sz")
    n_core = lax.axis_size("core")
    shard = seq_index()
    cosine, sine = rope_tables(positions)
    q_rot = (
        rotate(queries.astype(jnp.float32).reshape(length, heads, HD), cosine, sine, 1.0)
        .astype(jnp.bfloat16)
        .reshape(length, heads * HD)
    )
    k_rot = (
        rotate(keys.astype(jnp.float32).reshape(length, groups, HD), cosine, sine, 1.0)
        .astype(jnp.bfloat16)
        .reshape(length, groups * HD)
    )
    kv_count = lax.axis_size("kv")
    kv_me = lax.axis_index("kv")
    col_w = out_weight.shape[1]
    n_seq = seq_size()
    pieces = lax.all_to_all(out_weight, "kv", split_axis=0, concat_axis=1, tiled=True)
    stripes = lax.all_gather(pieces, SEQ, axis=1, tiled=True)
    og_list = [out_grad.reshape(length, n_seq, col_w)]
    for j in range(1, kv_count):
        got = lax.ppermute(out_grad, "kv", [(i, (i - j) % kv_count) for i in range(kv_count)])
        og_list.append(got.reshape(length, n_seq, col_w))
    og_stack = jnp.stack(og_list, axis=2)
    og_perm = jnp.roll(og_stack, kv_me, axis=2).reshape(length, -1)
    contract = (((1,), (1,)), ((), ()))
    head_grad = lax.dot_general(
        og_perm, stripes, contract, preferred_element_type=jnp.float32
    ).astype(jnp.bfloat16)
    width = keys.shape[1]
    doc_row = jnp.zeros((1, 2 * width), jnp.bfloat16).at[0, :length].set(
        doc_ids.astype(jnp.bfloat16)
    )
    packed = jnp.concatenate(
        [jnp.concatenate([k_rot, values], axis=1), doc_row], axis=0
    )[None]
    win = gather_window(packed)
    key_win = win[:, :length, :width].reshape(-1, width)
    value_win = win[:, :length, width:].reshape(-1, width)
    doc_win = win[:, length, :length].reshape(-1).astype(jnp.int32)
    blocks_dev = length // BLK
    mask_pad = jnp.pad(block_mask, ((0, 0), (REACH * blocks_dev, 0)))
    mask_rows = lax.dynamic_slice_in_dim(mask_pad, shard * blocks_dev, (REACH + 1) * blocks_dev, 1)
    allowed = allowed_mask(shard, doc_ids, doc_win, mask_rows)
    scale = HD ** (-0.5)
    q_grp = q_rot.reshape(length, per_group, HD)
    g_grp = head_grad.reshape(length, per_group, HD)
    scores = jnp.einsum("thd,ud->htu", q_grp, key_win, preferred_element_type=jnp.float32) * scale
    scores = jnp.where(allowed[None], scores, -1e30)
    top = jnp.max(scores, axis=2, keepdims=True)
    expo = jnp.exp(scores - top)
    weights = (expo / jnp.sum(expo, axis=2, keepdims=True)).astype(jnp.bfloat16)
    out_grp = jnp.einsum(
        "htu,ud->thd", weights, value_win, preferred_element_type=jnp.float32
    ).astype(jnp.bfloat16)
    delta = jnp.sum(g_grp.astype(jnp.float32) * out_grp.astype(jnp.float32), axis=2)
    dprob = jnp.einsum("thd,ud->htu", g_grp, value_win, preferred_element_type=jnp.float32)
    dscore = (weights.astype(jnp.float32) * (dprob - delta.T[:, :, None])).astype(jnp.bfloat16)
    dq_rot = jnp.einsum("htu,ud->thd", dscore, key_win, preferred_element_type=jnp.float32) * scale
    dkey_sum = jnp.einsum("htu,thd->ud", dscore, q_grp, preferred_element_type=jnp.float32) * scale
    dvalue_sum = jnp.einsum("htu,thd->ud", weights, g_grp, preferred_element_type=jnp.float32)
    attn = out_grp.reshape(length, per_group * HD)
    dkv = jnp.concatenate([dkey_sum, dvalue_sum], axis=1).reshape(REACH + 1, length, 2 * HD)
    attn, dkv = lax.optimization_barrier((attn, dkv))
    lo_part = jnp.einsum(
        "tr,rskj->ktsj",
        attn,
        stripes.reshape(attn.shape[1], n_seq, kv_count, col_w),
        preferred_element_type=jnp.float32,
    ).astype(jnp.bfloat16)
    total = lax.dynamic_index_in_dim(lo_part, kv_me, 0, keepdims=False).astype(jnp.float32)
    for j in range(1, kv_count):
        dest = (kv_me + j) % kv_count
        piece = lax.dynamic_index_in_dim(lo_part, dest, 0, keepdims=False)
        got = lax.ppermute(piece, "kv", [(i, (i + j) % kv_count) for i in range(kv_count)])
        total = total + got.astype(jnp.float32)
    layer_out = total.reshape(length, n_seq * col_w).astype(jnp.bfloat16)
    dkv_total = return_window(dkv)
    dk_total = dkv_total[:, :HD]
    dv_total = dkv_total[:, HD:]
    query_grad = rotate(dq_rot, cosine, sine, -1.0).astype(jnp.bfloat16).reshape(length, heads * HD)
    key_grad = (
        rotate(dk_total.reshape(length, groups, HD), cosine, sine, -1.0)
        .astype(jnp.bfloat16)
        .reshape(length, groups * HD)
    )
    value_grad = dv_total.astype(jnp.bfloat16)
    return (layer_out, query_grad, key_grad, value_grad)


def solution(mesh):
    n_seq, n_kv = mesh.devices.shape
    cores = 2 if n_seq % 2 == 0 else 1
    grid = Mesh(mesh.devices.reshape(n_seq // cores, cores, n_kv), ("sz", "core", "kv"))
    in_specs = (
        P(SEQ, "kv"),
        P(SEQ, "kv"),
        P(SEQ, "kv"),
        P(None, ("kv",) + SEQ),
        P(SEQ, "kv"),
        P(SEQ),
        P(SEQ, None),
        P(None, SEQ),
    )
    out_specs = (P(SEQ, "kv"), P(SEQ, "kv"), P(SEQ, "kv"), P(SEQ, "kv"))
    return jax.shard_map(
        per_device, mesh=grid, in_specs=in_specs, out_specs=out_specs, check_vma=False
    )
```

```python
import math

import jax
import jax.numpy as jnp
from jax import lax
from jax.sharding import Mesh
from jax.sharding import PartitionSpec as P

HD = 128
BLK = 128
REACH = 9

SEQ = ("sz", "core")

rope_base = 1000000.0


def seq_size():
    return lax.axis_size("sz") * lax.axis_size("core")


def seq_index():
    return lax.axis_index("sz") * lax.axis_size("core") + lax.axis_index("core")


def shifted(block, distance):
    count = seq_size()
    devices = range(count)
    route = [(i - distance, i) for i in devices if i - distance in devices]
    return lax.ppermute(block, SEQ, route)


def rope_tables(positions):
    pairs = HD // 2
    index = jnp.arange(pairs)
    inv_freq = jnp.exp(index.astype(jnp.float32) * (-2.0 * math.log(rope_base) / HD))
    temporal = HD // 8
    which = jnp.where(index >= pairs - temporal, 0, jnp.where(index % 2 == 0, 1, 2))
    places = positions.astype(jnp.float32)
    chosen = jnp.where((which == 0)[:, None], places[0][None, :], 0.0)
    chosen = chosen + jnp.where((which == 1)[:, None], places[1][None, :], 0.0)
    chosen = chosen + jnp.where((which == 2)[:, None], places[2][None, :], 0.0)
    angle = chosen.T * inv_freq[None, :]
    return (jnp.cos(angle), jnp.sin(angle))


def rotate(block, cosine, sine, sign):
    half = HD // 2
    first = block[..., :half]
    second = block[..., half:]
    cos_part = cosine[:, None, :]
    sin_part = sine[:, None, :] * sign
    return jnp.concatenate(
        [first * cos_part - second * sin_part, second * cos_part + first * sin_part], axis=-1
    )


def allowed_mask(shard, doc_query, doc_key, mask_rows):
    length = doc_query.shape[0]
    width = doc_key.shape[0]
    query_pos = shard * length + jnp.arange(length, dtype=jnp.int32)
    key_pos = (shard - REACH) * length + jnp.arange(width, dtype=jnp.int32)
    near = jnp.repeat(jnp.repeat(mask_rows, BLK, axis=0), BLK, axis=1) > 0
    same_block = query_pos[:, None] // BLK == key_pos[None, :] // BLK
    return (
        (doc_query[:, None] == doc_key[None, :])
        & (key_pos[None, :] <= query_pos[:, None])
        & (key_pos[None, :] >= 0)
        & (near | same_block)
    )


def attend(query, key_win, value_win, allowed, grad_out):
    scale = HD ** (-0.5)
    contract = (((1,), (1,)), ((), ()))
    columns = (((0,), (0,)), ((), ()))
    scores = lax.dot_general(query, key_win, contract, preferred_element_type=jnp.float32) * scale
    scores = jnp.where(allowed, scores, -1e30)
    top = jnp.max(scores, axis=1, keepdims=True)
    expo = jnp.exp(scores - top)
    weights = (expo / jnp.sum(expo, axis=1, keepdims=True)).astype(jnp.bfloat16)
    output = jnp.dot(weights, value_win, preferred_element_type=jnp.float32).astype(jnp.bfloat16)
    delta = jnp.sum(
        grad_out.astype(jnp.float32) * output.astype(jnp.float32), axis=1, keepdims=True
    )
    dprob = lax.dot_general(grad_out, value_win, contract, preferred_element_type=jnp.float32)
    dscore = (weights.astype(jnp.float32) * (dprob - delta)).astype(jnp.bfloat16)
    dquery = jnp.dot(dscore, key_win, preferred_element_type=jnp.float32) * scale
    dkey = lax.dot_general(dscore, query, columns, preferred_element_type=jnp.float32) * scale
    dvalue = lax.dot_general(weights, grad_out, columns, preferred_element_type=jnp.float32)
    return (output, dquery, dkey, dvalue)


def gather_window(packed):
    one = jnp.concatenate([shifted(packed, 1), packed], axis=0)
    two = jnp.concatenate([shifted(one, 2), one], axis=0)
    four = jnp.concatenate([shifted(two, 4), two], axis=0)
    far = shifted(one, 8)
    return jnp.concatenate([far, four], axis=0)


def return_window(pieces):
    far = shifted(pieces[:2].astype(jnp.bfloat16), -8).astype(jnp.float32)
    four = pieces[2:]
    two = four[4:] + shifted(four[:4].astype(jnp.bfloat16), -4).astype(jnp.float32)
    one = two[2:] + shifted(two[:2].astype(jnp.bfloat16), -2).astype(jnp.float32) + far
    return one[1] + shifted(one[:1].astype(jnp.bfloat16), -1).astype(jnp.float32)[0]


def per_device(queries, keys, values, out_weight, out_grad, doc_ids, block_mask, positions):
    length = queries.shape[0]
    groups = keys.shape[1] // HD
    heads = queries.shape[1] // HD
    per_group = heads // groups
    n_sz = lax.axis_size("sz")
    n_core = lax.axis_size("core")
    shard = seq_index()
    cosine, sine = rope_tables(positions)
    q_rot = (
        rotate(queries.astype(jnp.float32).reshape(length, heads, HD), cosine, sine, 1.0)
        .astype(jnp.bfloat16)
        .reshape(length, heads * HD)
    )
    k_rot = (
        rotate(keys.astype(jnp.float32).reshape(length, groups, HD), cosine, sine, 1.0)
        .astype(jnp.bfloat16)
        .reshape(length, groups * HD)
    )
    kv_count = lax.axis_size("kv")
    kv_me = lax.axis_index("kv")
    col_w = out_weight.shape[1]
    n_seq = seq_size()
    pieces = lax.all_to_all(out_weight, "kv", split_axis=0, concat_axis=1, tiled=True)
    rows = pieces.shape[0]
    p4 = pieces.reshape(rows, kv_count, col_w)
    n_ring = 2
    n_sc = kv_count - n_ring
    wa = lax.all_gather(p4[:, :n_sc].reshape(rows, n_sc * col_w), SEQ, axis=1, tiled=True)
    xb = p4[:, None, n_sc:]
    reach = 1
    while reach < n_seq:
        moved = lax.ppermute(xb, SEQ, [(i, (i + reach) % n_seq) for i in range(n_seq)])
        xb = jnp.concatenate([xb, moved], axis=1)
        reach *= 2
    og_list = [out_grad.reshape(length, n_seq, col_w)]
    for j in range(1, kv_count):
        got = lax.ppermute(out_grad, "kv", [(i, (i - j) % kv_count) for i in range(kv_count)])
        og_list.append(got.reshape(length, n_seq, col_w))
    og_stack = jnp.stack(og_list, axis=2)
    og4 = jnp.roll(og_stack, kv_me, axis=2)
    og_a = og4[:, :, :n_sc].reshape(length, -1)
    og_b = jnp.roll(og4[:, ::-1, n_sc:], shard + 1, axis=1)
    contract = (((1,), (1,)), ((), ()))
    hg_a = lax.dot_general(og_a, wa, contract, preferred_element_type=jnp.float32)
    hg_b = jnp.einsum("tonj,ronj->tr", og_b, xb, preferred_element_type=jnp.float32)
    head_grad = (hg_a + hg_b).astype(jnp.bfloat16)
    width = keys.shape[1]
    doc_row = jnp.zeros((1, 2 * width), jnp.bfloat16).at[0, :length].set(
        doc_ids.astype(jnp.bfloat16)
    )
    packed = jnp.concatenate(
        [jnp.concatenate([k_rot, values], axis=1), doc_row], axis=0
    )[None]
    win = gather_window(packed)
    key_win = win[:, :length, :width].reshape(-1, width)
    value_win = win[:, :length, width:].reshape(-1, width)
    doc_win = win[:, length, :length].reshape(-1).astype(jnp.int32)
    blocks_dev = length // BLK
    mask_pad = jnp.pad(block_mask, ((0, 0), (REACH * blocks_dev, 0)))
    mask_rows = lax.dynamic_slice_in_dim(mask_pad, shard * blocks_dev, (REACH + 1) * blocks_dev, 1)
    allowed = allowed_mask(shard, doc_ids, doc_win, mask_rows)
    scale = HD ** (-0.5)
    q_grp = q_rot.reshape(length, per_group, HD)
    g_grp = head_grad.reshape(length, per_group, HD)
    scores = jnp.einsum("thd,ud->htu", q_grp, key_win, preferred_element_type=jnp.float32) * scale
    scores = jnp.where(allowed[None], scores, -1e30)
    top = jnp.max(scores, axis=2, keepdims=True)
    expo = jnp.exp(scores - top)
    weights = (expo / jnp.sum(expo, axis=2, keepdims=True)).astype(jnp.bfloat16)
    out_grp = jnp.einsum(
        "htu,ud->thd", weights, value_win, preferred_element_type=jnp.float32
    ).astype(jnp.bfloat16)
    delta = jnp.sum(g_grp.astype(jnp.float32) * out_grp.astype(jnp.float32), axis=2)
    dprob = jnp.einsum("thd,ud->htu", g_grp, value_win, preferred_element_type=jnp.float32)
    dscore = (weights.astype(jnp.float32) * (dprob - delta.T[:, :, None])).astype(jnp.bfloat16)
    dq_rot = jnp.einsum("htu,ud->thd", dscore, key_win, preferred_element_type=jnp.float32) * scale
    dkey_sum = jnp.einsum("htu,thd->ud", dscore, q_grp, preferred_element_type=jnp.float32) * scale
    dvalue_sum = jnp.einsum("htu,thd->ud", weights, g_grp, preferred_element_type=jnp.float32)
    attn = out_grp.reshape(length, per_group * HD)
    dkv = jnp.concatenate([dkey_sum, dvalue_sum], axis=1).reshape(REACH + 1, length, 2 * HD)
    attn, dkv = lax.optimization_barrier((attn, dkv))
    lo_a = jnp.einsum(
        "tr,rskj->ktsj",
        attn,
        wa.reshape(rows, n_seq, n_sc, col_w),
        preferred_element_type=jnp.float32,
    )
    lo_b = jnp.einsum("tr,ronj->ntoj", attn, xb, preferred_element_type=jnp.float32)
    lo_b = jnp.roll(lo_b[:, :, ::-1], shard + 1, axis=2)
    lo_part = jnp.concatenate([lo_a, lo_b], axis=0).astype(jnp.bfloat16)
    total = lax.dynamic_index_in_dim(lo_part, kv_me, 0, keepdims=False).astype(jnp.float32)
    for j in range(1, kv_count):
        dest = (kv_me + j) % kv_count
        piece = lax.dynamic_index_in_dim(lo_part, dest, 0, keepdims=False)
        got = lax.ppermute(piece, "kv", [(i, (i + j) % kv_count) for i in range(kv_count)])
        total = total + got.astype(jnp.float32)
    layer_out = total.reshape(length, n_seq * col_w).astype(jnp.bfloat16)
    dkv_total = return_window(dkv)
    dk_total = dkv_total[:, :HD]
    dv_total = dkv_total[:, HD:]
    query_grad = rotate(dq_rot, cosine, sine, -1.0).astype(jnp.bfloat16).reshape(length, heads * HD)
    key_grad = (
        rotate(dk_total.reshape(length, groups, HD), cosine, sine, -1.0)
        .astype(jnp.bfloat16)
        .reshape(length, groups * HD)
    )
    value_grad = dv_total.astype(jnp.bfloat16)
    return (layer_out, query_grad, key_grad, value_grad)


def solution(mesh):
    n_seq, n_kv = mesh.devices.shape
    cores = 2 if n_seq % 2 == 0 else 1
    grid = Mesh(mesh.devices.reshape(n_seq // cores, cores, n_kv), ("sz", "core", "kv"))
    in_specs = (
        P(SEQ, "kv"),
        P(SEQ, "kv"),
        P(SEQ, "kv"),
        P(None, ("kv",) + SEQ),
        P(SEQ, "kv"),
        P(SEQ),
        P(SEQ, None),
        P(None, SEQ),
    )
    out_specs = (P(SEQ, "kv"), P(SEQ, "kv"), P(SEQ, "kv"), P(SEQ, "kv"))
    return jax.shard_map(
        per_device, mesh=grid, in_specs=in_specs, out_specs=out_specs, check_vma=False
    )
```

```python
import math

import jax
import jax.numpy as jnp
from jax import lax
from jax.sharding import Mesh
from jax.sharding import PartitionSpec as P

HD = 128
BLK = 128
REACH = 9

SEQ = ("sz", "core")

rope_base = 1000000.0


def seq_size():
    return lax.axis_size("sz") * lax.axis_size("core")


def seq_index():
    return lax.axis_index("sz") * lax.axis_size("core") + lax.axis_index("core")


def shifted(block, distance):
    count = seq_size()
    devices = range(count)
    route = [(i - distance, i) for i in devices if i - distance in devices]
    return lax.ppermute(block, SEQ, route)


def rope_tables(positions):
    pairs = HD // 2
    index = jnp.arange(pairs)
    inv_freq = jnp.exp(index.astype(jnp.float32) * (-2.0 * math.log(rope_base) / HD))
    temporal = HD // 8
    which = jnp.where(index >= pairs - temporal, 0, jnp.where(index % 2 == 0, 1, 2))
    places = positions.astype(jnp.float32)
    chosen = jnp.where((which == 0)[:, None], places[0][None, :], 0.0)
    chosen = chosen + jnp.where((which == 1)[:, None], places[1][None, :], 0.0)
    chosen = chosen + jnp.where((which == 2)[:, None], places[2][None, :], 0.0)
    angle = chosen.T * inv_freq[None, :]
    return (jnp.cos(angle), jnp.sin(angle))


def rotate(block, cosine, sine, sign):
    half = HD // 2
    first = block[..., :half]
    second = block[..., half:]
    cos_part = cosine[:, None, :]
    sin_part = sine[:, None, :] * sign
    return jnp.concatenate(
        [first * cos_part - second * sin_part, second * cos_part + first * sin_part], axis=-1
    )


def allowed_mask(shard, doc_query, doc_key, mask_rows):
    length = doc_query.shape[0]
    width = doc_key.shape[0]
    query_pos = shard * length + jnp.arange(length, dtype=jnp.int32)
    key_pos = (shard - REACH) * length + jnp.arange(width, dtype=jnp.int32)
    near = jnp.repeat(jnp.repeat(mask_rows, BLK, axis=0), BLK, axis=1) > 0
    same_block = query_pos[:, None] // BLK == key_pos[None, :] // BLK
    return (
        (doc_query[:, None] == doc_key[None, :])
        & (key_pos[None, :] <= query_pos[:, None])
        & (key_pos[None, :] >= 0)
        & (near | same_block)
    )


def attend(query, key_win, value_win, allowed, grad_out):
    scale = HD ** (-0.5)
    contract = (((1,), (1,)), ((), ()))
    columns = (((0,), (0,)), ((), ()))
    scores = lax.dot_general(query, key_win, contract, preferred_element_type=jnp.float32) * scale
    scores = jnp.where(allowed, scores, -1e30)
    top = jnp.max(scores, axis=1, keepdims=True)
    expo = jnp.exp(scores - top)
    weights = (expo / jnp.sum(expo, axis=1, keepdims=True)).astype(jnp.bfloat16)
    output = jnp.dot(weights, value_win, preferred_element_type=jnp.float32).astype(jnp.bfloat16)
    delta = jnp.sum(
        grad_out.astype(jnp.float32) * output.astype(jnp.float32), axis=1, keepdims=True
    )
    dprob = lax.dot_general(grad_out, value_win, contract, preferred_element_type=jnp.float32)
    dscore = (weights.astype(jnp.float32) * (dprob - delta)).astype(jnp.bfloat16)
    dquery = jnp.dot(dscore, key_win, preferred_element_type=jnp.float32) * scale
    dkey = lax.dot_general(dscore, query, columns, preferred_element_type=jnp.float32) * scale
    dvalue = lax.dot_general(weights, grad_out, columns, preferred_element_type=jnp.float32)
    return (output, dquery, dkey, dvalue)


def gather_window(packed):
    one = jnp.concatenate([shifted(packed, 1), packed], axis=0)
    two = jnp.concatenate([shifted(one, 2), one], axis=0)
    four = jnp.concatenate([shifted(two, 4), two], axis=0)
    far = shifted(one, 8)
    return jnp.concatenate([far, four], axis=0)


def return_window(pieces):
    far = shifted(pieces[:2].astype(jnp.bfloat16), -8).astype(jnp.float32)
    four = pieces[2:]
    two = four[4:] + shifted(four[:4].astype(jnp.bfloat16), -4).astype(jnp.float32)
    one = two[2:] + shifted(two[:2].astype(jnp.bfloat16), -2).astype(jnp.float32) + far
    return one[1] + shifted(one[:1].astype(jnp.bfloat16), -1).astype(jnp.float32)[0]


def per_device(queries, keys, values, out_weight, out_grad, doc_ids, block_mask, positions):
    length = queries.shape[0]
    groups = keys.shape[1] // HD
    heads = queries.shape[1] // HD
    per_group = heads // groups
    n_sz = lax.axis_size("sz")
    n_core = lax.axis_size("core")
    shard = seq_index()
    cosine, sine = rope_tables(positions)
    q_rot = (
        rotate(queries.astype(jnp.float32).reshape(length, heads, HD), cosine, sine, 1.0)
        .astype(jnp.bfloat16)
        .reshape(length, heads * HD)
    )
    k_rot = (
        rotate(keys.astype(jnp.float32).reshape(length, groups, HD), cosine, sine, 1.0)
        .astype(jnp.bfloat16)
        .reshape(length, groups * HD)
    )
    kv_count = lax.axis_size("kv")
    kv_me = lax.axis_index("kv")
    col_w = out_weight.shape[1]
    n_seq = seq_size()
    pieces = lax.all_to_all(out_weight, "kv", split_axis=0, concat_axis=1, tiled=True)
    stripes = lax.all_gather(pieces, SEQ, axis=1, tiled=True)
    og_list = [out_grad.reshape(length, n_seq, col_w)]
    for j in range(1, kv_count):
        got = lax.ppermute(out_grad, "kv", [(i, (i - j) % kv_count) for i in range(kv_count)])
        og_list.append(got.reshape(length, n_seq, col_w))
    og_stack = jnp.stack(og_list, axis=2)
    og_perm = jnp.roll(og_stack, kv_me, axis=2).reshape(length, -1)
    contract = (((1,), (1,)), ((), ()))
    head_grad = lax.dot_general(
        og_perm, stripes, contract, preferred_element_type=jnp.float32
    ).astype(jnp.bfloat16)
    width = keys.shape[1]
    doc_row = jnp.zeros((1, 2 * width), jnp.bfloat16).at[0, :length].set(
        doc_ids.astype(jnp.bfloat16)
    )
    packed = jnp.concatenate(
        [jnp.concatenate([k_rot, values], axis=1), doc_row], axis=0
    )[None]
    win = gather_window(packed)
    key_win = win[:, :length, :width].reshape(-1, width)
    value_win = win[:, :length, width:].reshape(-1, width)
    doc_win = win[:, length, :length].reshape(-1).astype(jnp.int32)
    blocks_dev = length // BLK
    mask_pad = jnp.pad(block_mask, ((0, 0), (REACH * blocks_dev, 0)))
    mask_rows = lax.dynamic_slice_in_dim(mask_pad, shard * blocks_dev, (REACH + 1) * blocks_dev, 1)
    allowed = allowed_mask(shard, doc_ids, doc_win, mask_rows)
    scale = HD ** (-0.5)
    q_grp = q_rot.reshape(length, per_group, HD)
    g_grp = head_grad.reshape(length, per_group, HD)
    scores = jnp.einsum("thd,ud->htu", q_grp, key_win, preferred_element_type=jnp.float32) * scale
    scores = jnp.where(allowed[None], scores, -1e30)
    top = jnp.max(scores, axis=2, keepdims=True)
    expo = jnp.exp(scores - top)
    weights = (expo / jnp.sum(expo, axis=2, keepdims=True)).astype(jnp.bfloat16)
    out_grp = jnp.einsum(
        "htu,ud->thd", weights, value_win, preferred_element_type=jnp.float32
    ).astype(jnp.bfloat16)
    delta = jnp.sum(g_grp.astype(jnp.float32) * out_grp.astype(jnp.float32), axis=2)
    dprob = jnp.einsum("thd,ud->htu", g_grp, value_win, preferred_element_type=jnp.float32)
    dscore = (weights.astype(jnp.float32) * (dprob - delta.T[:, :, None])).astype(jnp.bfloat16)
    dq_rot = jnp.einsum("htu,ud->thd", dscore, key_win, preferred_element_type=jnp.float32) * scale
    dkey_sum = jnp.einsum("htu,thd->ud", dscore, q_grp, preferred_element_type=jnp.float32) * scale
    dvalue_sum = jnp.einsum("htu,thd->ud", weights, g_grp, preferred_element_type=jnp.float32)
    attn = out_grp.reshape(length, per_group * HD)
    dkv = jnp.concatenate([dkey_sum, dvalue_sum], axis=1).reshape(REACH + 1, length, 2 * HD)
    attn, dkv = lax.optimization_barrier((attn, dkv))
    lo_part = jnp.einsum(
        "tr,rskj->ktsj",
        attn,
        stripes.reshape(attn.shape[1], n_seq, kv_count, col_w),
        preferred_element_type=jnp.float32,
    ).astype(jnp.bfloat16)
    got = lax.all_to_all(lo_part, "kv", split_axis=0, concat_axis=0, tiled=True)
    total = jnp.sum(got.astype(jnp.float32), axis=0)
    layer_out = total.reshape(length, n_seq * col_w).astype(jnp.bfloat16)
    dkv_total = return_window(dkv)
    dk_total = dkv_total[:, :HD]
    dv_total = dkv_total[:, HD:]
    query_grad = rotate(dq_rot, cosine, sine, -1.0).astype(jnp.bfloat16).reshape(length, heads * HD)
    key_grad = (
        rotate(dk_total.reshape(length, groups, HD), cosine, sine, -1.0)
        .astype(jnp.bfloat16)
        .reshape(length, groups * HD)
    )
    value_grad = dv_total.astype(jnp.bfloat16)
    return (layer_out, query_grad, key_grad, value_grad)


def solution(mesh):
    n_seq, n_kv = mesh.devices.shape
    cores = 2 if n_seq % 2 == 0 else 1
    grid = Mesh(mesh.devices.reshape(n_seq // cores, cores, n_kv), ("sz", "core", "kv"))
    in_specs = (
        P(SEQ, "kv"),
        P(SEQ, "kv"),
        P(SEQ, "kv"),
        P(None, ("kv",) + SEQ),
        P(SEQ, "kv"),
        P(SEQ),
        P(SEQ, None),
        P(None, SEQ),
    )
    out_specs = (P(SEQ, "kv"), P(SEQ, "kv"), P(SEQ, "kv"), P(SEQ, "kv"))
    return jax.shard_map(
        per_device, mesh=grid, in_specs=in_specs, out_specs=out_specs, check_vma=False
    )
```

```python
import math

import jax
import jax.numpy as jnp
from jax import lax
from jax.sharding import Mesh
from jax.sharding import PartitionSpec as P

HD = 128
BLK = 128
REACH = 9

SEQ = ("sz", "core")

rope_base = 1000000.0


def seq_size():
    return lax.axis_size("sz") * lax.axis_size("core")


def seq_index():
    return lax.axis_index("sz") * lax.axis_size("core") + lax.axis_index("core")


def shifted(block, distance):
    count = seq_size()
    devices = range(count)
    route = [(i - distance, i) for i in devices if i - distance in devices]
    return lax.ppermute(block, SEQ, route)


def rope_tables(positions):
    pairs = HD // 2
    index = jnp.arange(pairs)
    inv_freq = jnp.exp(index.astype(jnp.float32) * (-2.0 * math.log(rope_base) / HD))
    temporal = HD // 8
    which = jnp.where(index >= pairs - temporal, 0, jnp.where(index % 2 == 0, 1, 2))
    places = positions.astype(jnp.float32)
    chosen = jnp.where((which == 0)[:, None], places[0][None, :], 0.0)
    chosen = chosen + jnp.where((which == 1)[:, None], places[1][None, :], 0.0)
    chosen = chosen + jnp.where((which == 2)[:, None], places[2][None, :], 0.0)
    angle = chosen.T * inv_freq[None, :]
    return (jnp.cos(angle), jnp.sin(angle))


def rotate(block, cosine, sine, sign):
    half = HD // 2
    first = block[..., :half]
    second = block[..., half:]
    cos_part = cosine[:, None, :]
    sin_part = sine[:, None, :] * sign
    return jnp.concatenate(
        [first * cos_part - second * sin_part, second * cos_part + first * sin_part], axis=-1
    )


def allowed_mask(shard, doc_query, doc_key, mask_rows):
    length = doc_query.shape[0]
    width = doc_key.shape[0]
    query_pos = shard * length + jnp.arange(length, dtype=jnp.int32)
    key_pos = (shard - REACH) * length + jnp.arange(width, dtype=jnp.int32)
    near = jnp.repeat(jnp.repeat(mask_rows, BLK, axis=0), BLK, axis=1) > 0
    same_block = query_pos[:, None] // BLK == key_pos[None, :] // BLK
    return (
        (doc_query[:, None] == doc_key[None, :])
        & (key_pos[None, :] <= query_pos[:, None])
        & (key_pos[None, :] >= 0)
        & (near | same_block)
    )


def attend(query, key_win, value_win, allowed, grad_out):
    scale = HD ** (-0.5)
    contract = (((1,), (1,)), ((), ()))
    columns = (((0,), (0,)), ((), ()))
    scores = lax.dot_general(query, key_win, contract, preferred_element_type=jnp.float32) * scale
    scores = jnp.where(allowed, scores, -1e30)
    top = jnp.max(scores, axis=1, keepdims=True)
    expo = jnp.exp(scores - top)
    weights = (expo / jnp.sum(expo, axis=1, keepdims=True)).astype(jnp.bfloat16)
    output = jnp.dot(weights, value_win, preferred_element_type=jnp.float32).astype(jnp.bfloat16)
    delta = jnp.sum(
        grad_out.astype(jnp.float32) * output.astype(jnp.float32), axis=1, keepdims=True
    )
    dprob = lax.dot_general(grad_out, value_win, contract, preferred_element_type=jnp.float32)
    dscore = (weights.astype(jnp.float32) * (dprob - delta)).astype(jnp.bfloat16)
    dquery = jnp.dot(dscore, key_win, preferred_element_type=jnp.float32) * scale
    dkey = lax.dot_general(dscore, query, columns, preferred_element_type=jnp.float32) * scale
    dvalue = lax.dot_general(weights, grad_out, columns, preferred_element_type=jnp.float32)
    return (output, dquery, dkey, dvalue)


def gather_window(packed):
    one = jnp.concatenate([shifted(packed, 1), packed], axis=0)
    two = jnp.concatenate([shifted(one, 2), one], axis=0)
    four = jnp.concatenate([shifted(two, 4), two], axis=0)
    far = shifted(one, 8)
    return jnp.concatenate([far, four], axis=0)


def return_window(pieces):
    def send(block, distance):
        return shifted(block.astype(jnp.bfloat16), -distance).astype(jnp.float32)

    acc = pieces[REACH - 2 : REACH + 1][::-1]
    acc = acc + send(pieces[REACH - 5 : REACH - 2][::-1], 3)
    acc = acc + send(pieces[REACH - 8 : REACH - 5][::-1], 6)
    first = acc[0] + send(pieces[REACH - 9 : REACH - 8], 9)[0]
    return first + send(acc[1], 1) + send(acc[2], 2)


def per_device(queries, keys, values, out_weight, out_grad, doc_ids, block_mask, positions):
    length = queries.shape[0]
    groups = keys.shape[1] // HD
    heads = queries.shape[1] // HD
    per_group = heads // groups
    n_sz = lax.axis_size("sz")
    n_core = lax.axis_size("core")
    shard = seq_index()
    cosine, sine = rope_tables(positions)
    q_rot = (
        rotate(queries.astype(jnp.float32).reshape(length, heads, HD), cosine, sine, 1.0)
        .astype(jnp.bfloat16)
        .reshape(length, heads * HD)
    )
    k_rot = (
        rotate(keys.astype(jnp.float32).reshape(length, groups, HD), cosine, sine, 1.0)
        .astype(jnp.bfloat16)
        .reshape(length, groups * HD)
    )
    kv_count = lax.axis_size("kv")
    kv_me = lax.axis_index("kv")
    col_w = out_weight.shape[1]
    n_seq = seq_size()
    pieces = lax.all_to_all(out_weight, "kv", split_axis=0, concat_axis=1, tiled=True)
    stripes = lax.all_gather(pieces, SEQ, axis=1, tiled=True)
    og_list = [out_grad.reshape(length, n_seq, col_w)]
    for j in range(1, kv_count):
        got = lax.ppermute(out_grad, "kv", [(i, (i - j) % kv_count) for i in range(kv_count)])
        og_list.append(got.reshape(length, n_seq, col_w))
    og_stack = jnp.stack(og_list, axis=2)
    og_perm = jnp.roll(og_stack, kv_me, axis=2).reshape(length, -1)
    contract = (((1,), (1,)), ((), ()))
    head_grad = lax.dot_general(
        og_perm, stripes, contract, preferred_element_type=jnp.float32
    ).astype(jnp.bfloat16)
    width = keys.shape[1]
    doc_row = jnp.zeros((1, 2 * width), jnp.bfloat16).at[0, :length].set(
        doc_ids.astype(jnp.bfloat16)
    )
    packed = jnp.concatenate(
        [jnp.concatenate([k_rot, values], axis=1), doc_row], axis=0
    )[None]
    win = gather_window(packed)
    key_win = win[:, :length, :width].reshape(-1, width)
    value_win = win[:, :length, width:].reshape(-1, width)
    doc_win = win[:, length, :length].reshape(-1).astype(jnp.int32)
    blocks_dev = length // BLK
    mask_pad = jnp.pad(block_mask, ((0, 0), (REACH * blocks_dev, 0)))
    mask_rows = lax.dynamic_slice_in_dim(mask_pad, shard * blocks_dev, (REACH + 1) * blocks_dev, 1)
    allowed = allowed_mask(shard, doc_ids, doc_win, mask_rows)
    scale = HD ** (-0.5)
    q_grp = q_rot.reshape(length, per_group, HD)
    g_grp = head_grad.reshape(length, per_group, HD)
    scores = jnp.einsum("thd,ud->htu", q_grp, key_win, preferred_element_type=jnp.float32) * scale
    scores = jnp.where(allowed[None], scores, -1e30)
    top = jnp.max(scores, axis=2, keepdims=True)
    expo = jnp.exp(scores - top)
    weights = (expo / jnp.sum(expo, axis=2, keepdims=True)).astype(jnp.bfloat16)
    out_grp = jnp.einsum(
        "htu,ud->thd", weights, value_win, preferred_element_type=jnp.float32
    ).astype(jnp.bfloat16)
    delta = jnp.sum(g_grp.astype(jnp.float32) * out_grp.astype(jnp.float32), axis=2)
    dprob = jnp.einsum("thd,ud->htu", g_grp, value_win, preferred_element_type=jnp.float32)
    dscore = (weights.astype(jnp.float32) * (dprob - delta.T[:, :, None])).astype(jnp.bfloat16)
    dq_rot = jnp.einsum("htu,ud->thd", dscore, key_win, preferred_element_type=jnp.float32) * scale
    dkey_sum = jnp.einsum("htu,thd->ud", dscore, q_grp, preferred_element_type=jnp.float32) * scale
    dvalue_sum = jnp.einsum("htu,thd->ud", weights, g_grp, preferred_element_type=jnp.float32)
    attn = out_grp.reshape(length, per_group * HD)
    dkv = jnp.concatenate([dkey_sum, dvalue_sum], axis=1).reshape(REACH + 1, length, 2 * HD)
    attn, dkv = lax.optimization_barrier((attn, dkv))
    lo_part = jnp.einsum(
        "tr,rskj->ktsj",
        attn,
        stripes.reshape(attn.shape[1], n_seq, kv_count, col_w),
        preferred_element_type=jnp.float32,
    ).astype(jnp.bfloat16)
    total = lax.dynamic_index_in_dim(lo_part, kv_me, 0, keepdims=False).astype(jnp.float32)
    for j in range(1, kv_count):
        dest = (kv_me + j) % kv_count
        piece = lax.dynamic_index_in_dim(lo_part, dest, 0, keepdims=False)
        got = lax.ppermute(piece, "kv", [(i, (i + j) % kv_count) for i in range(kv_count)])
        total = total + got.astype(jnp.float32)
    layer_out = total.reshape(length, n_seq * col_w).astype(jnp.bfloat16)
    dkv_total = return_window(dkv)
    dk_total = dkv_total[:, :HD]
    dv_total = dkv_total[:, HD:]
    query_grad = rotate(dq_rot, cosine, sine, -1.0).astype(jnp.bfloat16).reshape(length, heads * HD)
    key_grad = (
        rotate(dk_total.reshape(length, groups, HD), cosine, sine, -1.0)
        .astype(jnp.bfloat16)
        .reshape(length, groups * HD)
    )
    value_grad = dv_total.astype(jnp.bfloat16)
    return (layer_out, query_grad, key_grad, value_grad)


def solution(mesh):
    n_seq, n_kv = mesh.devices.shape
    cores = 2 if n_seq % 2 == 0 else 1
    grid = Mesh(mesh.devices.reshape(n_seq // cores, cores, n_kv), ("sz", "core", "kv"))
    in_specs = (
        P(SEQ, "kv"),
        P(SEQ, "kv"),
        P(SEQ, "kv"),
        P(None, ("kv",) + SEQ),
        P(SEQ, "kv"),
        P(SEQ),
        P(SEQ, None),
        P(None, SEQ),
    )
    out_specs = (P(SEQ, "kv"), P(SEQ, "kv"), P(SEQ, "kv"), P(SEQ, "kv"))
    return jax.shard_map(
        per_device, mesh=grid, in_specs=in_specs, out_specs=out_specs, check_vma=False
    )
```

```python
import math

import jax
import jax.numpy as jnp
from jax import lax
from jax.sharding import Mesh
from jax.sharding import PartitionSpec as P

HD = 128
BLK = 128
REACH = 9

SEQ = ("sz", "core")

rope_base = 1000000.0


def seq_size():
    return lax.axis_size("sz") * lax.axis_size("core")


def seq_index():
    return lax.axis_index("sz") * lax.axis_size("core") + lax.axis_index("core")


def shifted(block, distance):
    count = seq_size()
    devices = range(count)
    route = [(i - distance, i) for i in devices if i - distance in devices]
    return lax.ppermute(block, SEQ, route)


def rope_tables(positions):
    pairs = HD // 2
    index = jnp.arange(pairs)
    inv_freq = jnp.exp(index.astype(jnp.float32) * (-2.0 * math.log(rope_base) / HD))
    temporal = HD // 8
    which = jnp.where(index >= pairs - temporal, 0, jnp.where(index % 2 == 0, 1, 2))
    places = positions.astype(jnp.float32)
    chosen = jnp.where((which == 0)[:, None], places[0][None, :], 0.0)
    chosen = chosen + jnp.where((which == 1)[:, None], places[1][None, :], 0.0)
    chosen = chosen + jnp.where((which == 2)[:, None], places[2][None, :], 0.0)
    angle = chosen.T * inv_freq[None, :]
    return (jnp.cos(angle), jnp.sin(angle))


def rotate(block, cosine, sine, sign):
    half = HD // 2
    first = block[..., :half]
    second = block[..., half:]
    cos_part = cosine[:, None, :]
    sin_part = sine[:, None, :] * sign
    return jnp.concatenate(
        [first * cos_part - second * sin_part, second * cos_part + first * sin_part], axis=-1
    )


def allowed_mask(shard, doc_query, doc_key, mask_rows):
    length = doc_query.shape[0]
    width = doc_key.shape[0]
    query_pos = shard * length + jnp.arange(length, dtype=jnp.int32)
    key_pos = (shard - REACH) * length + jnp.arange(width, dtype=jnp.int32)
    near = jnp.repeat(jnp.repeat(mask_rows, BLK, axis=0), BLK, axis=1) > 0
    same_block = query_pos[:, None] // BLK == key_pos[None, :] // BLK
    return (
        (doc_query[:, None] == doc_key[None, :])
        & (key_pos[None, :] <= query_pos[:, None])
        & (key_pos[None, :] >= 0)
        & (near | same_block)
    )


def attend(query, key_win, value_win, allowed, grad_out):
    scale = HD ** (-0.5)
    contract = (((1,), (1,)), ((), ()))
    columns = (((0,), (0,)), ((), ()))
    scores = lax.dot_general(query, key_win, contract, preferred_element_type=jnp.float32) * scale
    scores = jnp.where(allowed, scores, -1e30)
    top = jnp.max(scores, axis=1, keepdims=True)
    expo = jnp.exp(scores - top)
    weights = (expo / jnp.sum(expo, axis=1, keepdims=True)).astype(jnp.bfloat16)
    output = jnp.dot(weights, value_win, preferred_element_type=jnp.float32).astype(jnp.bfloat16)
    delta = jnp.sum(
        grad_out.astype(jnp.float32) * output.astype(jnp.float32), axis=1, keepdims=True
    )
    dprob = lax.dot_general(grad_out, value_win, contract, preferred_element_type=jnp.float32)
    dscore = (weights.astype(jnp.float32) * (dprob - delta)).astype(jnp.bfloat16)
    dquery = jnp.dot(dscore, key_win, preferred_element_type=jnp.float32) * scale
    dkey = lax.dot_general(dscore, query, columns, preferred_element_type=jnp.float32) * scale
    dvalue = lax.dot_general(weights, grad_out, columns, preferred_element_type=jnp.float32)
    return (output, dquery, dkey, dvalue)


def gather_window(packed):
    one = jnp.concatenate([shifted(packed, 1), packed], axis=0)
    two = jnp.concatenate([shifted(one, 2), one], axis=0)
    four = jnp.concatenate([shifted(two, 4), two], axis=0)
    far = shifted(one, 8)
    return jnp.concatenate([far, four], axis=0)


def return_window(pieces):
    far = shifted(pieces[:2].astype(jnp.bfloat16), -8).astype(jnp.float32)
    four = pieces[2:]
    two = four[4:] + shifted(four[:4].astype(jnp.bfloat16), -4).astype(jnp.float32)
    one = two[2:] + shifted(two[:2].astype(jnp.bfloat16), -2).astype(jnp.float32) + far
    return one[1] + shifted(one[:1].astype(jnp.bfloat16), -1).astype(jnp.float32)[0]


def per_device(queries, keys, values, out_weight, out_grad, doc_ids, block_mask, positions):
    length = queries.shape[0]
    groups = keys.shape[1] // HD
    heads = queries.shape[1] // HD
    per_group = heads // groups
    n_sz = lax.axis_size("sz")
    n_core = lax.axis_size("core")
    shard = seq_index()
    cosine, sine = rope_tables(positions)
    q_rot = (
        rotate(queries.astype(jnp.float32).reshape(length, heads, HD), cosine, sine, 1.0)
        .astype(jnp.bfloat16)
        .reshape(length, heads * HD)
    )
    k_rot = (
        rotate(keys.astype(jnp.float32).reshape(length, groups, HD), cosine, sine, 1.0)
        .astype(jnp.bfloat16)
        .reshape(length, groups * HD)
    )
    kv_count = lax.axis_size("kv")
    kv_me = lax.axis_index("kv")
    col_w = out_weight.shape[1]
    n_seq = seq_size()
    rows_w = out_weight.shape[0] // kv_count
    w_got = [lax.dynamic_slice_in_dim(out_weight, kv_me * rows_w, rows_w, 0)]
    for j in range(1, kv_count):
        block = lax.dynamic_slice_in_dim(out_weight, ((kv_me + j) % kv_count) * rows_w, rows_w, 0)
        w_got.append(lax.ppermute(block, "kv", [(i, (i + j) % kv_count) for i in range(kv_count)]))
    pieces = jnp.roll(jnp.stack(w_got, axis=1)[:, ::-1], kv_me + 1, axis=1).reshape(rows_w, -1)
    stripes = lax.all_gather(pieces, SEQ, axis=1, tiled=True)
    og_list = [out_grad.reshape(length, n_seq, col_w)]
    for j in range(1, kv_count):
        got = lax.ppermute(out_grad, "kv", [(i, (i - j) % kv_count) for i in range(kv_count)])
        og_list.append(got.reshape(length, n_seq, col_w))
    og_stack = jnp.stack(og_list, axis=2)
    og_perm = jnp.roll(og_stack, kv_me, axis=2).reshape(length, -1)
    contract = (((1,), (1,)), ((), ()))
    head_grad = lax.dot_general(
        og_perm, stripes, contract, preferred_element_type=jnp.float32
    ).astype(jnp.bfloat16)
    width = keys.shape[1]
    doc_row = jnp.zeros((1, 2 * width), jnp.bfloat16).at[0, :length].set(
        doc_ids.astype(jnp.bfloat16)
    )
    packed = jnp.concatenate(
        [jnp.concatenate([k_rot, values], axis=1), doc_row], axis=0
    )[None]
    win = gather_window(packed)
    key_win = win[:, :length, :width].reshape(-1, width)
    value_win = win[:, :length, width:].reshape(-1, width)
    doc_win = win[:, length, :length].reshape(-1).astype(jnp.int32)
    blocks_dev = length // BLK
    mask_pad = jnp.pad(block_mask, ((0, 0), (REACH * blocks_dev, 0)))
    mask_rows = lax.dynamic_slice_in_dim(mask_pad, shard * blocks_dev, (REACH + 1) * blocks_dev, 1)
    allowed = allowed_mask(shard, doc_ids, doc_win, mask_rows)
    scale = HD ** (-0.5)
    q_grp = q_rot.reshape(length, per_group, HD)
    g_grp = head_grad.reshape(length, per_group, HD)
    scores = jnp.einsum("thd,ud->htu", q_grp, key_win, preferred_element_type=jnp.float32) * scale
    scores = jnp.where(allowed[None], scores, -1e30)
    top = jnp.max(scores, axis=2, keepdims=True)
    expo = jnp.exp(scores - top)
    weights = (expo / jnp.sum(expo, axis=2, keepdims=True)).astype(jnp.bfloat16)
    out_grp = jnp.einsum(
        "htu,ud->thd", weights, value_win, preferred_element_type=jnp.float32
    ).astype(jnp.bfloat16)
    delta = jnp.sum(g_grp.astype(jnp.float32) * out_grp.astype(jnp.float32), axis=2)
    dprob = jnp.einsum("thd,ud->htu", g_grp, value_win, preferred_element_type=jnp.float32)
    dscore = (weights.astype(jnp.float32) * (dprob - delta.T[:, :, None])).astype(jnp.bfloat16)
    dq_rot = jnp.einsum("htu,ud->thd", dscore, key_win, preferred_element_type=jnp.float32) * scale
    dkey_sum = jnp.einsum("htu,thd->ud", dscore, q_grp, preferred_element_type=jnp.float32) * scale
    dvalue_sum = jnp.einsum("htu,thd->ud", weights, g_grp, preferred_element_type=jnp.float32)
    attn = out_grp.reshape(length, per_group * HD)
    dkv = jnp.concatenate([dkey_sum, dvalue_sum], axis=1).reshape(REACH + 1, length, 2 * HD)
    attn, dkv = lax.optimization_barrier((attn, dkv))
    lo_part = jnp.einsum(
        "tr,rskj->ktsj",
        attn,
        stripes.reshape(attn.shape[1], n_seq, kv_count, col_w),
        preferred_element_type=jnp.float32,
    ).astype(jnp.bfloat16)
    total = lax.dynamic_index_in_dim(lo_part, kv_me, 0, keepdims=False).astype(jnp.float32)
    for j in range(1, kv_count):
        dest = (kv_me + j) % kv_count
        piece = lax.dynamic_index_in_dim(lo_part, dest, 0, keepdims=False)
        got = lax.ppermute(piece, "kv", [(i, (i + j) % kv_count) for i in range(kv_count)])
        total = total + got.astype(jnp.float32)
    layer_out = total.reshape(length, n_seq * col_w).astype(jnp.bfloat16)
    dkv_total = return_window(dkv)
    dk_total = dkv_total[:, :HD]
    dv_total = dkv_total[:, HD:]
    query_grad = rotate(dq_rot, cosine, sine, -1.0).astype(jnp.bfloat16).reshape(length, heads * HD)
    key_grad = (
        rotate(dk_total.reshape(length, groups, HD), cosine, sine, -1.0)
        .astype(jnp.bfloat16)
        .reshape(length, groups * HD)
    )
    value_grad = dv_total.astype(jnp.bfloat16)
    return (layer_out, query_grad, key_grad, value_grad)


def solution(mesh):
    n_seq, n_kv = mesh.devices.shape
    cores = 2 if n_seq % 2 == 0 else 1
    grid = Mesh(mesh.devices.reshape(n_seq // cores, cores, n_kv), ("sz", "core", "kv"))
    in_specs = (
        P(SEQ, "kv"),
        P(SEQ, "kv"),
        P(SEQ, "kv"),
        P(None, ("kv",) + SEQ),
        P(SEQ, "kv"),
        P(SEQ),
        P(SEQ, None),
        P(None, SEQ),
    )
    out_specs = (P(SEQ, "kv"), P(SEQ, "kv"), P(SEQ, "kv"), P(SEQ, "kv"))
    return jax.shard_map(
        per_device, mesh=grid, in_specs=in_specs, out_specs=out_specs, check_vma=False
    )
```

```python
import math

import jax
import jax.numpy as jnp
from jax import lax
from jax.sharding import Mesh
from jax.sharding import PartitionSpec as P

HD = 128
BLK = 128
REACH = 9

SEQ = ("sz", "core")

rope_base = 1000000.0


def seq_size():
    return lax.axis_size("sz") * lax.axis_size("core")


def seq_index():
    return lax.axis_index("sz") * lax.axis_size("core") + lax.axis_index("core")


def shifted(block, distance):
    count = seq_size()
    devices = range(count)
    route = [(i - distance, i) for i in devices if i - distance in devices]
    return lax.ppermute(block, SEQ, route)


def rope_tables(positions):
    pairs = HD // 2
    index = jnp.arange(pairs)
    inv_freq = jnp.exp(index.astype(jnp.float32) * (-2.0 * math.log(rope_base) / HD))
    temporal = HD // 8
    which = jnp.where(index >= pairs - temporal, 0, jnp.where(index % 2 == 0, 1, 2))
    places = positions.astype(jnp.float32)
    chosen = jnp.where((which == 0)[:, None], places[0][None, :], 0.0)
    chosen = chosen + jnp.where((which == 1)[:, None], places[1][None, :], 0.0)
    chosen = chosen + jnp.where((which == 2)[:, None], places[2][None, :], 0.0)
    angle = chosen.T * inv_freq[None, :]
    return (jnp.cos(angle), jnp.sin(angle))


def rotate(block, cosine, sine, sign):
    half = HD // 2
    first = block[..., :half]
    second = block[..., half:]
    cos_part = cosine[:, None, :]
    sin_part = sine[:, None, :] * sign
    return jnp.concatenate(
        [first * cos_part - second * sin_part, second * cos_part + first * sin_part], axis=-1
    )


def allowed_mask(shard, doc_query, doc_key, mask_rows):
    length = doc_query.shape[0]
    width = doc_key.shape[0]
    query_pos = shard * length + jnp.arange(length, dtype=jnp.int32)
    key_pos = (shard - REACH) * length + jnp.arange(width, dtype=jnp.int32)
    near = jnp.repeat(jnp.repeat(mask_rows, BLK, axis=0), BLK, axis=1) > 0
    same_block = query_pos[:, None] // BLK == key_pos[None, :] // BLK
    return (
        (doc_query[:, None] == doc_key[None, :])
        & (key_pos[None, :] <= query_pos[:, None])
        & (key_pos[None, :] >= 0)
        & (near | same_block)
    )


def attend(query, key_win, value_win, allowed, grad_out):
    scale = HD ** (-0.5)
    contract = (((1,), (1,)), ((), ()))
    columns = (((0,), (0,)), ((), ()))
    scores = lax.dot_general(query, key_win, contract, preferred_element_type=jnp.float32) * scale
    scores = jnp.where(allowed, scores, -1e30)
    top = jnp.max(scores, axis=1, keepdims=True)
    expo = jnp.exp(scores - top)
    weights = (expo / jnp.sum(expo, axis=1, keepdims=True)).astype(jnp.bfloat16)
    output = jnp.dot(weights, value_win, preferred_element_type=jnp.float32).astype(jnp.bfloat16)
    delta = jnp.sum(
        grad_out.astype(jnp.float32) * output.astype(jnp.float32), axis=1, keepdims=True
    )
    dprob = lax.dot_general(grad_out, value_win, contract, preferred_element_type=jnp.float32)
    dscore = (weights.astype(jnp.float32) * (dprob - delta)).astype(jnp.bfloat16)
    dquery = jnp.dot(dscore, key_win, preferred_element_type=jnp.float32) * scale
    dkey = lax.dot_general(dscore, query, columns, preferred_element_type=jnp.float32) * scale
    dvalue = lax.dot_general(weights, grad_out, columns, preferred_element_type=jnp.float32)
    return (output, dquery, dkey, dvalue)


def gather_window(packed):
    one = jnp.concatenate([shifted(packed, 1), packed], axis=0)
    two = jnp.concatenate([shifted(one, 2), one], axis=0)
    four = jnp.concatenate([shifted(two, 4), two], axis=0)
    far = shifted(one, 8)
    return jnp.concatenate([far, four], axis=0)


def return_window(pieces, held):
    far = shifted(pieces[:2].astype(jnp.bfloat16), -8).astype(jnp.float32)
    four = pieces[2:]
    two = four[4:] + shifted(four[:4].astype(jnp.bfloat16), -4).astype(jnp.float32)
    one = two[2:] + shifted(two[:2].astype(jnp.bfloat16), -2).astype(jnp.float32) + far
    total = one[1] + shifted(one[:1].astype(jnp.bfloat16), -1).astype(jnp.float32)[0]
    one, held = lax.optimization_barrier((one, held))
    return total, held


def per_device(queries, keys, values, out_weight, out_grad, doc_ids, block_mask, positions):
    length = queries.shape[0]
    groups = keys.shape[1] // HD
    heads = queries.shape[1] // HD
    per_group = heads // groups
    n_sz = lax.axis_size("sz")
    n_core = lax.axis_size("core")
    shard = seq_index()
    cosine, sine = rope_tables(positions)
    q_rot = (
        rotate(queries.astype(jnp.float32).reshape(length, heads, HD), cosine, sine, 1.0)
        .astype(jnp.bfloat16)
        .reshape(length, heads * HD)
    )
    k_rot = (
        rotate(keys.astype(jnp.float32).reshape(length, groups, HD), cosine, sine, 1.0)
        .astype(jnp.bfloat16)
        .reshape(length, groups * HD)
    )
    kv_count = lax.axis_size("kv")
    kv_me = lax.axis_index("kv")
    col_w = out_weight.shape[1]
    n_seq = seq_size()
    pieces = lax.all_to_all(out_weight, "kv", split_axis=0, concat_axis=1, tiled=True)
    stripes = lax.all_gather(pieces, SEQ, axis=1, tiled=True)
    og_list = [out_grad.reshape(length, n_seq, col_w)]
    for j in range(1, kv_count):
        got = lax.ppermute(out_grad, "kv", [(i, (i - j) % kv_count) for i in range(kv_count)])
        og_list.append(got.reshape(length, n_seq, col_w))
    og_stack = jnp.stack(og_list, axis=2)
    og_perm = jnp.roll(og_stack, kv_me, axis=2).reshape(length, -1)
    contract = (((1,), (1,)), ((), ()))
    head_grad = lax.dot_general(
        og_perm, stripes, contract, preferred_element_type=jnp.float32
    ).astype(jnp.bfloat16)
    width = keys.shape[1]
    doc_row = jnp.zeros((1, 2 * width), jnp.bfloat16).at[0, :length].set(
        doc_ids.astype(jnp.bfloat16)
    )
    packed = jnp.concatenate(
        [jnp.concatenate([k_rot, values], axis=1), doc_row], axis=0
    )[None]
    win = gather_window(packed)
    key_win = win[:, :length, :width].reshape(-1, width)
    value_win = win[:, :length, width:].reshape(-1, width)
    doc_win = win[:, length, :length].reshape(-1).astype(jnp.int32)
    blocks_dev = length // BLK
    mask_pad = jnp.pad(block_mask, ((0, 0), (REACH * blocks_dev, 0)))
    mask_rows = lax.dynamic_slice_in_dim(mask_pad, shard * blocks_dev, (REACH + 1) * blocks_dev, 1)
    allowed = allowed_mask(shard, doc_ids, doc_win, mask_rows)
    scale = HD ** (-0.5)
    q_grp = q_rot.reshape(length, per_group, HD)
    g_grp = head_grad.reshape(length, per_group, HD)
    scores = jnp.einsum("thd,ud->htu", q_grp, key_win, preferred_element_type=jnp.float32) * scale
    scores = jnp.where(allowed[None], scores, -1e30)
    top = jnp.max(scores, axis=2, keepdims=True)
    expo = jnp.exp(scores - top)
    weights = (expo / jnp.sum(expo, axis=2, keepdims=True)).astype(jnp.bfloat16)
    out_grp = jnp.einsum(
        "htu,ud->thd", weights, value_win, preferred_element_type=jnp.float32
    ).astype(jnp.bfloat16)
    delta = jnp.sum(g_grp.astype(jnp.float32) * out_grp.astype(jnp.float32), axis=2)
    dprob = jnp.einsum("thd,ud->htu", g_grp, value_win, preferred_element_type=jnp.float32)
    dscore = (weights.astype(jnp.float32) * (dprob - delta.T[:, :, None])).astype(jnp.bfloat16)
    dq_rot = jnp.einsum("htu,ud->thd", dscore, key_win, preferred_element_type=jnp.float32) * scale
    dkey_sum = jnp.einsum("htu,thd->ud", dscore, q_grp, preferred_element_type=jnp.float32) * scale
    dvalue_sum = jnp.einsum("htu,thd->ud", weights, g_grp, preferred_element_type=jnp.float32)
    attn = out_grp.reshape(length, per_group * HD)
    dkv = jnp.concatenate([dkey_sum, dvalue_sum], axis=1).reshape(REACH + 1, length, 2 * HD)
    attn, dkv = lax.optimization_barrier((attn, dkv))
    lo_part = jnp.einsum(
        "tr,rskj->ktsj",
        attn,
        stripes.reshape(attn.shape[1], n_seq, kv_count, col_w),
        preferred_element_type=jnp.float32,
    ).astype(jnp.bfloat16)
    dkv_total, lo_part = return_window(dkv, lo_part)
    total = lax.dynamic_index_in_dim(lo_part, kv_me, 0, keepdims=False).astype(jnp.float32)
    for j in range(1, kv_count):
        dest = (kv_me + j) % kv_count
        piece = lax.dynamic_index_in_dim(lo_part, dest, 0, keepdims=False)
        got = lax.ppermute(piece, "kv", [(i, (i + j) % kv_count) for i in range(kv_count)])
        total = total + got.astype(jnp.float32)
    layer_out = total.reshape(length, n_seq * col_w).astype(jnp.bfloat16)
    dk_total = dkv_total[:, :HD]
    dv_total = dkv_total[:, HD:]
    query_grad = rotate(dq_rot, cosine, sine, -1.0).astype(jnp.bfloat16).reshape(length, heads * HD)
    key_grad = (
        rotate(dk_total.reshape(length, groups, HD), cosine, sine, -1.0)
        .astype(jnp.bfloat16)
        .reshape(length, groups * HD)
    )
    value_grad = dv_total.astype(jnp.bfloat16)
    return (layer_out, query_grad, key_grad, value_grad)


def solution(mesh):
    n_seq, n_kv = mesh.devices.shape
    cores = 2 if n_seq % 2 == 0 else 1
    grid = Mesh(mesh.devices.reshape(n_seq // cores, cores, n_kv), ("sz", "core", "kv"))
    in_specs = (
        P(SEQ, "kv"),
        P(SEQ, "kv"),
        P(SEQ, "kv"),
        P(None, ("kv",) + SEQ),
        P(SEQ, "kv"),
        P(SEQ),
        P(SEQ, None),
        P(None, SEQ),
    )
    out_specs = (P(SEQ, "kv"), P(SEQ, "kv"), P(SEQ, "kv"), P(SEQ, "kv"))
    return jax.shard_map(
        per_device, mesh=grid, in_specs=in_specs, out_specs=out_specs, check_vma=False
    )
```

```python
import math

import jax
import jax.numpy as jnp
from jax import lax
from jax.sharding import Mesh
from jax.sharding import PartitionSpec as P

HD = 128
BLK = 128
REACH = 9

SEQ = ("sz", "core")

rope_base = 1000000.0


def seq_size():
    return lax.axis_size("sz") * lax.axis_size("core")


def seq_index():
    return lax.axis_index("sz") * lax.axis_size("core") + lax.axis_index("core")


def shifted(block, distance):
    count = seq_size()
    devices = range(count)
    route = [(i - distance, i) for i in devices if i - distance in devices]
    return lax.ppermute(block, SEQ, route)


def rope_tables(positions):
    pairs = HD // 2
    index = jnp.arange(pairs)
    inv_freq = jnp.exp(index.astype(jnp.float32) * (-2.0 * math.log(rope_base) / HD))
    temporal = HD // 8
    which = jnp.where(index >= pairs - temporal, 0, jnp.where(index % 2 == 0, 1, 2))
    places = positions.astype(jnp.float32)
    chosen = jnp.where((which == 0)[:, None], places[0][None, :], 0.0)
    chosen = chosen + jnp.where((which == 1)[:, None], places[1][None, :], 0.0)
    chosen = chosen + jnp.where((which == 2)[:, None], places[2][None, :], 0.0)
    angle = chosen.T * inv_freq[None, :]
    return (jnp.cos(angle), jnp.sin(angle))


def rotate(block, cosine, sine, sign):
    half = HD // 2
    first = block[..., :half]
    second = block[..., half:]
    cos_part = cosine[:, None, :]
    sin_part = sine[:, None, :] * sign
    return jnp.concatenate(
        [first * cos_part - second * sin_part, second * cos_part + first * sin_part], axis=-1
    )


def allowed_mask(shard, doc_query, doc_key, mask_rows):
    length = doc_query.shape[0]
    width = doc_key.shape[0]
    query_pos = shard * length + jnp.arange(length, dtype=jnp.int32)
    key_pos = (shard - REACH) * length + jnp.arange(width, dtype=jnp.int32)
    near = jnp.repeat(jnp.repeat(mask_rows, BLK, axis=0), BLK, axis=1) > 0
    same_block = query_pos[:, None] // BLK == key_pos[None, :] // BLK
    return (
        (doc_query[:, None] == doc_key[None, :])
        & (key_pos[None, :] <= query_pos[:, None])
        & (key_pos[None, :] >= 0)
        & (near | same_block)
    )


def attend(query, key_win, value_win, allowed, grad_out):
    scale = HD ** (-0.5)
    contract = (((1,), (1,)), ((), ()))
    columns = (((0,), (0,)), ((), ()))
    scores = lax.dot_general(query, key_win, contract, preferred_element_type=jnp.float32) * scale
    scores = jnp.where(allowed, scores, -1e30)
    top = jnp.max(scores, axis=1, keepdims=True)
    expo = jnp.exp(scores - top)
    weights = (expo / jnp.sum(expo, axis=1, keepdims=True)).astype(jnp.bfloat16)
    output = jnp.dot(weights, value_win, preferred_element_type=jnp.float32).astype(jnp.bfloat16)
    delta = jnp.sum(
        grad_out.astype(jnp.float32) * output.astype(jnp.float32), axis=1, keepdims=True
    )
    dprob = lax.dot_general(grad_out, value_win, contract, preferred_element_type=jnp.float32)
    dscore = (weights.astype(jnp.float32) * (dprob - delta)).astype(jnp.bfloat16)
    dquery = jnp.dot(dscore, key_win, preferred_element_type=jnp.float32) * scale
    dkey = lax.dot_general(dscore, query, columns, preferred_element_type=jnp.float32) * scale
    dvalue = lax.dot_general(weights, grad_out, columns, preferred_element_type=jnp.float32)
    return (output, dquery, dkey, dvalue)


def gather_window(packed):
    one = jnp.concatenate([shifted(packed, 1), packed], axis=0)
    two = jnp.concatenate([shifted(one, 2), one], axis=0)
    four = jnp.concatenate([shifted(two, 4), two], axis=0)
    far = shifted(one, 8)
    return jnp.concatenate([far, four], axis=0)


def return_window(pieces):
    far = shifted(pieces[:2].astype(jnp.bfloat16), -8).astype(jnp.float32)
    four = pieces[2:]
    two = four[4:] + shifted(four[:4].astype(jnp.bfloat16), -4).astype(jnp.float32)
    one = two[2:] + shifted(two[:2].astype(jnp.bfloat16), -2).astype(jnp.float32) + far
    return one[1] + shifted(one[:1].astype(jnp.bfloat16), -1).astype(jnp.float32)[0]


def per_device(queries, keys, values, out_weight, out_grad, doc_ids, block_mask, positions):
    length = queries.shape[0]
    groups = keys.shape[1] // HD
    heads = queries.shape[1] // HD
    per_group = heads // groups
    n_sz = lax.axis_size("sz")
    n_core = lax.axis_size("core")
    shard = seq_index()
    cosine, sine = rope_tables(positions)
    q_rot = (
        rotate(queries.astype(jnp.float32).reshape(length, heads, HD), cosine, sine, 1.0)
        .astype(jnp.bfloat16)
        .reshape(length, heads * HD)
    )
    k_rot = (
        rotate(keys.astype(jnp.float32).reshape(length, groups, HD), cosine, sine, 1.0)
        .astype(jnp.bfloat16)
        .reshape(length, groups * HD)
    )
    kv_count = lax.axis_size("kv")
    kv_me = lax.axis_index("kv")
    col_w = out_weight.shape[1]
    n_seq = seq_size()
    pieces = lax.all_to_all(out_weight, "kv", split_axis=0, concat_axis=1, tiled=True)
    stripes = lax.all_gather(pieces, SEQ, axis=1, tiled=True)
    og_list = [out_grad.reshape(length, n_seq, col_w)]
    for j in range(1, kv_count):
        got = lax.ppermute(out_grad, "kv", [(i, (i - j) % kv_count) for i in range(kv_count)])
        og_list.append(got.reshape(length, n_seq, col_w))
    og_stack = jnp.stack(og_list, axis=2)
    og_perm = jnp.roll(og_stack, kv_me, axis=2).reshape(length, -1)
    contract = (((1,), (1,)), ((), ()))
    head_grad = lax.dot_general(
        og_perm, stripes, contract, preferred_element_type=jnp.float32
    ).astype(jnp.bfloat16)
    width = keys.shape[1]
    doc_row = jnp.zeros((1, 2 * width), jnp.bfloat16).at[0, :length].set(
        doc_ids.astype(jnp.bfloat16)
    )
    packed = jnp.concatenate(
        [jnp.concatenate([k_rot, values], axis=1), doc_row], axis=0
    )[None]
    win = gather_window(packed)
    key_win = win[:, :length, :width].reshape(-1, width)
    value_win = win[:, :length, width:].reshape(-1, width)
    doc_win = win[:, length, :length].reshape(-1).astype(jnp.int32)
    blocks_dev = length // BLK
    mask_pad = jnp.pad(block_mask, ((0, 0), (REACH * blocks_dev, 0)))
    mask_rows = lax.dynamic_slice_in_dim(mask_pad, shard * blocks_dev, (REACH + 1) * blocks_dev, 1)
    allowed = allowed_mask(shard, doc_ids, doc_win, mask_rows)
    scale = HD ** (-0.5)
    q_grp = q_rot.reshape(length, per_group, HD)
    g_grp = head_grad.reshape(length, per_group, HD)
    scores = jnp.einsum("thd,ud->htu", q_grp, key_win, preferred_element_type=jnp.float32) * scale
    scores = jnp.where(allowed[None], scores, -1e30)
    top = jnp.max(scores, axis=2, keepdims=True)
    expo = jnp.exp(scores - top)
    weights = (expo / jnp.sum(expo, axis=2, keepdims=True)).astype(jnp.bfloat16)
    out_grp = jnp.einsum(
        "htu,ud->thd", weights, value_win, preferred_element_type=jnp.float32
    ).astype(jnp.bfloat16)
    delta = jnp.sum(g_grp.astype(jnp.float32) * out_grp.astype(jnp.float32), axis=2)
    dprob = jnp.einsum("thd,ud->htu", g_grp, value_win, preferred_element_type=jnp.float32)
    dscore = (weights.astype(jnp.float32) * (dprob - delta.T[:, :, None])).astype(jnp.bfloat16)
    dq_rot = jnp.einsum("htu,ud->thd", dscore, key_win, preferred_element_type=jnp.float32) * scale
    dkey_sum = jnp.einsum("htu,thd->ud", dscore, q_grp, preferred_element_type=jnp.float32) * scale
    dvalue_sum = jnp.einsum("htu,thd->ud", weights, g_grp, preferred_element_type=jnp.float32)
    attn = out_grp.reshape(length, per_group * HD)
    dkv = jnp.concatenate([dkey_sum, dvalue_sum], axis=1).reshape(REACH + 1, length, 2 * HD)
    attn, dkv = lax.optimization_barrier((attn, dkv))
    lo_part = jnp.einsum(
        "tr,rskj->ktsj",
        attn,
        stripes.reshape(attn.shape[1], n_seq, kv_count, col_w),
        preferred_element_type=jnp.float32,
    ).astype(jnp.bfloat16)
    total = lax.dynamic_index_in_dim(lo_part, kv_me, 0, keepdims=False).astype(jnp.float32)
    for j in range(kv_count - 1, 0, -1):
        dest = (kv_me + j) % kv_count
        piece = lax.dynamic_index_in_dim(lo_part, dest, 0, keepdims=False)
        got = lax.ppermute(piece, "kv", [(i, (i + j) % kv_count) for i in range(kv_count)])
        total = total + got.astype(jnp.float32)
    layer_out = total.reshape(length, n_seq * col_w).astype(jnp.bfloat16)
    dkv_total = return_window(dkv)
    dk_total = dkv_total[:, :HD]
    dv_total = dkv_total[:, HD:]
    query_grad = rotate(dq_rot, cosine, sine, -1.0).astype(jnp.bfloat16).reshape(length, heads * HD)
    key_grad = (
        rotate(dk_total.reshape(length, groups, HD), cosine, sine, -1.0)
        .astype(jnp.bfloat16)
        .reshape(length, groups * HD)
    )
    value_grad = dv_total.astype(jnp.bfloat16)
    return (layer_out, query_grad, key_grad, value_grad)


def solution(mesh):
    n_seq, n_kv = mesh.devices.shape
    cores = 2 if n_seq % 2 == 0 else 1
    grid = Mesh(mesh.devices.reshape(n_seq // cores, cores, n_kv), ("sz", "core", "kv"))
    in_specs = (
        P(SEQ, "kv"),
        P(SEQ, "kv"),
        P(SEQ, "kv"),
        P(None, ("kv",) + SEQ),
        P(SEQ, "kv"),
        P(SEQ),
        P(SEQ, None),
        P(None, SEQ),
    )
    out_specs = (P(SEQ, "kv"), P(SEQ, "kv"), P(SEQ, "kv"), P(SEQ, "kv"))
    return jax.shard_map(
        per_device, mesh=grid, in_specs=in_specs, out_specs=out_specs, check_vma=False
    )
```
